512 devices in a mesh: tok: 64 (over z_hi, y, x), head: 8 (over z_lo, core).
Axes of the slice: x: 4, y: 4, z: 16 (z_hi: 4, z_lo: 4; z = z_hi * 4 + z_lo), core: 2. Of those that a mesh axis runs over, the one named last changes fastest.
Arguments:
- hidden_in: bfloat16 [16384, 2560], P('tok'), may hold values from -6 to 6
- norm_gain: float32 [2560], replicated, may hold values from 0.1 to 1.9
- w_qkv: bfloat16 [2560, 3840], P('tok', 'head'), may hold values from -4 to 4
- w_out: bfloat16 [2560, 2560], P('head', 'tok'), may hold values from -0.625 to 0.625
- prefill_cache: bfloat16 [8, 4096, 8, 1280], P(None, 'tok', 'head'), may hold values from -6 to 6
- lengths: int32 [8], replicated, may hold values from 1 to 4096, 20480 in all
- prefill_table: int32 [4096], replicated, may hold values from 0 to 4095, as said below
- decode_table: int32 [4096], replicated, may hold values from 0 to 4095, as said below
Outputs:
- attn_out: bfloat16 [16384, 2560], P('tok', 'head')
- decode_cache: bfloat16 [8, 4096, 8, 1280], P(None, 'tok', 'head')
The draws below stay inside these ranges and needn't reach their ends.
Inputs may be any that keep to these rules, and one draw needn't show every extreme that they name: `prefill_table`: each prefill slot holds exactly one logical block. `decode_table`: the block in prefill slot s * 64 + k goes to decode slot d * 64 + k, where d - s modulo the size of tok depends only on k and each residue occurs for exactly 1 values of k.
All inputs are finite; a program needn't handle non-finite values.
Results may differ from the reference program's by a relative error of at most 0.015.
The reference program's roundings to bfloat16 on the way (of `normed`, `queries`, `key_rows`, `values`, `weights` and `context`) count: a program that leaves them out, or rounds other values in their place, can miss the bound.
Values may be sent and summed in bfloat16 or wider, within the bound.
A program may use at most 64 MiB of HBM per device.

```python
import math
import jax
import jax.numpy as jnp
import numpy as np
from jax import lax

D = 2560
QH = 32
KVH = 8
HD = 80
QPK = 4
TOKENS = 16384
LAYERS = 8
BLK = 8
MAXLEN = 4096
REQS = 8
BPR = 512
NBLOCKS = 4096
PB = 64
CAP = 1


def table_pair(key):
    placed = jax.random.permutation(jax.random.fold_in(key, 11), NBLOCKS).astype(jnp.int32)
    devices = PB // CAP
    offsets = (jax.random.permutation(jax.random.fold_in(key, 12), PB) % devices).astype(jnp.int32)
    source = placed // PB
    within = placed % PB
    return (placed, (source + offsets[within]) % devices * PB + within)


def draw_prefill_table(key, part):
    return table_pair(key)[0]


def draw_decode_table(key, part):
    return table_pair(key)[1]


def draw_w_qkv(key, part):
    entries = jax.random.normal(key, (D, KVH, QPK + 2, HD), jnp.float32) * D ** (-0.5)
    entries = jnp.clip(entries, -4.0, 4.0)
    return entries.reshape(D, KVH * (QPK + 2) * HD).astype(jnp.bfloat16)


def levels(stream_key, shape, shards, low, top_value):
    factor_of, own = 1.0, jax.random.fold_in(stream_key, 6)
    for position, shards_of in shards:
        heights = jnp.exp(jax.random.uniform(jax.random.fold_in(own, position), (shards_of,), jnp.float32, low / len(shards), top_value / len(shards)))
        factor_of = factor_of * jnp.repeat(heights, shape[position] // shards_of).reshape([-1 if axis == position else 1 for axis in range(len(shape))])
    return factor_of


def length_profile(amount, total, most, slope):
    weights = [(1 << 20) // math.isqrt(standing ** slope) + 1 for standing in range(2, amount + 1)]
    surplus, given = total - most - (amount - 1), [1] * (amount - 1)
    while surplus > 0:
        movable = [i for i in range(amount - 1) if given[i] < most]
        mass, remaining = sum([weights[i] for i in movable]), surplus
        for i in movable:
            addition = min(most - given[i], max(1, remaining * weights[i] // mass), surplus)
            given[i] = given[i] + addition
            surplus = surplus - addition
    return np.array([most] + given)


def uneven_parts(stream_key, amount, total, reach, skew):
    if amount == 2:
        one = jax.random.randint(stream_key, (), max(1, total - reach), min(reach, total - 1) + 1)
        return jnp.stack([one, total - one])
    sizes = jnp.asarray(length_profile(amount, total, reach, skew), jnp.int32)
    twos = (amount - 1) // 2
    source_of, taker = sizes[1:1 + 2 * twos:2], sizes[2:2 + 2 * twos:2]
    margin = jnp.minimum(source_of - 1, reach - taker)
    passed = jax.random.randint(jax.random.fold_in(stream_key, 1), (twos,), 0, 1 << 20) % (margin + 1)
    sizes = sizes.at[1:1 + 2 * twos:2].set(source_of - passed).at[2:2 + 2 * twos:2].set(taker + passed)
    return sizes[jax.random.permutation(jax.random.fold_in(stream_key, 2), amount)]


def noise(rng, shape, spread, most, shards=(), kind=jnp.bfloat16):
    drawn = spread * jax.random.normal(rng, shape, jnp.float32)
    if shards:
        drawn = drawn * levels(rng, shape, shards, -0.22, 0.18)
    return jnp.clip(drawn, -most, most).astype(kind)


def setup_inputs(seed: int = 0) -> dict:
    keys = jax.random.split(jax.random.key(seed), 9)
    return {
        "hidden_in": noise(keys[0], (TOKENS, D), 1.0, 6.0, ((0, 64),)),
        "norm_gain": jnp.clip(1.0 + 0.18 * jax.random.normal(keys[1], (D,), jnp.float32), 0.1, 1.9),
        "w_qkv": draw_w_qkv(jax.random.fold_in(keys[8], 71), 0),
        "w_out": noise(keys[3], (QH * HD, D), HD ** -0.5, 0.625, ((0, 8), (1, 64))),
        "prefill_cache": noise(keys[4], (LAYERS, NBLOCKS, KVH, BLK * 2 * HD), 1.0, 6.0, ((1, 64), (2, 8))),
        "lengths": uneven_parts(keys[5], REQS, REQS * MAXLEN * 5 // 8, MAXLEN, 2).astype(jnp.int32),
        "prefill_table": draw_prefill_table(jax.random.fold_in(keys[8], 71), 0),
        "decode_table": draw_decode_table(jax.random.fold_in(keys[8], 71), 0),
    }


NORM_EPS = 1e-05
ROPE_BASE = 1000000.0

def rotary(vectors, positions):
    half_width = vectors.shape[-1] // 2
    frequency = ROPE_BASE ** (-2.0 * jnp.arange(half_width, dtype=jnp.float32) / vectors.shape[-1])
    angles = positions.astype(jnp.float32)[:, None] * frequency[None, :]
    cosine = jnp.cos(angles)[:, None, :]
    sines = jnp.sin(angles)[:, None, :]
    front_half = vectors[..., :half_width]
    back_half = vectors[..., half_width:]
    return jnp.concatenate([front_half * cosine - back_half * sines, back_half * cosine + front_half * sines], axis=-1)

def reference(hidden_in, norm_gain, w_qkv, w_out, prefill_cache, lengths, prefill_table, decode_table):
    float_rows = hidden_in.astype(jnp.float32)
    normed = (float_rows * lax.rsqrt(lax.optimization_barrier(jnp.mean(float_rows * float_rows, axis=-1, keepdims=True)) + NORM_EPS) * norm_gain).astype(jnp.bfloat16)
    projected = jnp.dot(normed, w_qkv, preferred_element_type=jnp.float32).reshape(TOKENS, KVH, QPK + 2, HD)
    positions = jnp.arange(TOKENS, dtype=jnp.int32)
    queries = rotary(projected[:, :, :QPK].reshape(TOKENS, KVH * QPK, HD), positions).astype(jnp.bfloat16)
    key_rows = rotary(projected[:, :, QPK], positions).astype(jnp.bfloat16)
    values = projected[:, :, QPK + 1].astype(jnp.bfloat16)
    block_rows = math.gcd(TOKENS, 512)
    block_count = TOKENS // block_rows
    query_groups = queries.reshape(block_count, block_rows, KVH, QPK, HD).transpose(2, 0, 3, 1, 4).reshape(KVH * block_count, QPK, block_rows, HD)
    keys_by_head = key_rows.transpose(1, 0, 2)
    values_by_head = values.transpose(1, 0, 2)
    scale_factor = 1.0 / math.sqrt(HD)

    def attend_block(entry):
        query_block, item_index = entry
        group = item_index // block_count
        block_start = item_index % block_count * block_rows
        key_float = keys_by_head[group].astype(jnp.float32)
        value_float = values_by_head[group].astype(jnp.float32)
        scores = jnp.einsum('jqd,kd->jqk', query_block.astype(jnp.float32), key_float) * scale_factor
        query_pos = block_start + jnp.arange(block_rows, dtype=jnp.int32)
        allowed = (positions[None, :] <= query_pos[:, None])[None]
        masked = jnp.where(allowed, scores, -1e+30)
        highest = lax.optimization_barrier(jnp.max(masked, axis=-1, keepdims=True))
        expo_terms = jnp.where(allowed, jnp.exp(masked - highest), 0.0)
        denominator = lax.optimization_barrier(jnp.sum(expo_terms, axis=-1, keepdims=True))
        weights = lax.optimization_barrier(expo_terms.astype(jnp.bfloat16))
        context = jnp.einsum('jqk,kd->jqd', weights.astype(jnp.float32), value_float) / denominator
        return context.astype(jnp.bfloat16)
    context = lax.map(attend_block, (query_groups, jnp.arange(KVH * block_count, dtype=jnp.int32)))
    context = context.reshape(KVH, block_count, QPK, block_rows, HD).transpose(1, 3, 0, 2, 4).reshape(TOKENS, QH * HD)
    attn_out = jnp.dot(context, w_out, preferred_element_type=jnp.float32).astype(jnp.bfloat16)
    logical = jnp.arange(NBLOCKS, dtype=jnp.int32)
    request = logical // BPR
    block_start = logical % BPR * BLK
    live = block_start[:, None] + jnp.arange(BLK, dtype=jnp.int32)[None, :] < lengths[request][:, None]
    moved = prefill_cache[:, prefill_table].reshape(LAYERS, NBLOCKS, KVH, BLK, 2 * HD)
    moved = moved * live[None, :, None, :, None].astype(jnp.bfloat16)
    moved = moved.reshape(LAYERS, NBLOCKS, KVH, BLK * 2 * HD)
    decode_cache = jnp.zeros_like(prefill_cache).at[:, decode_table].set(moved)
    return (attn_out, decode_cache)
```

```python
import functools
import math

import jax
import jax.numpy as jnp
from jax import lax
from jax.experimental import pallas as pl
from jax.experimental.pallas import tpu as pltpu
from jax.sharding import PartitionSpec as P

HD = 80
QPK = 4
BLK = 8
LANES = 128
SIDE = 4

NORM_EPS = 1e-05
ROPE_BASE = 1000000.0
LOWEST = -1e30
EXP2_SCALE = math.log2(math.e) / math.sqrt(HD)

MESH = pl.DeviceIdType.MESH


def coordinates():
    index = lax.axis_index("tok")
    return index // 16, (index // 4) % 4, index % 4


def along(axis, step):
    place = list(coordinates())
    place[axis] = (place[axis] + step) % SIDE
    return (place[0] * SIDE + place[1]) * SIDE + place[2]


def greet(far):
    barrier = pltpu.get_barrier_semaphore()
    peers = [along(axis, step) for axis in range(3) for step in (1, 3)]
    peers += [along(axis, 2) for axis in far]
    for peer in peers:
        pl.semaphore_signal(barrier, inc=1, device_id={"tok": peer}, device_id_type=MESH)
    pl.semaphore_wait(barrier, len(peers))


def remote(src, dst, send_sem, recv_sem, peer):
    return pltpu.make_async_remote_copy(
        src_ref=src,
        dst_ref=dst,
        send_sem=send_sem,
        recv_sem=recv_sem,
        device_id={"tok": peer},
        device_id_type=MESH,
    )


ORDERS = ((0, 1, 2), (0, 2, 1))


class Gather:
    def __init__(self, src, buf, split, send_sem, recv_sem, own_sem):
        self.src, self.buf, self.split = src, buf, split
        self.send_sem, self.recv_sem, self.own_sem = send_sem, recv_sem, own_sem
        self.sent = []

    def own(self):
        z, y, x = coordinates()
        for part in range(2):
            pltpu.make_async_copy(
                self.src.at[part], self.buf.at[part, z, y, x], self.own_sem.at[part]
            ).start()
        for part in range(2):
            pltpu.make_async_copy(
                self.src.at[part], self.buf.at[part, z, y, x], self.own_sem.at[part]
            ).wait()

    def view(self, part, phase, step, rows):
        done = ORDERS[part][:phase]
        axis = ORDERS[part][phase]
        place = list(coordinates())
        place[axis] = (place[axis] + step) % SIDE
        for seen in done:
            place[seen] = slice(None)
        return self.buf.at[(part, *place, rows, slice(None))]

    def copy(self, part, phase, which):
        axis = ORDERS[part][phase]
        every = slice(None)
        upper, lower = pl.ds(0, self.split), pl.ds(self.split, self.buf.shape[4] - self.split)
        step, rows, way = (
            (0, every, 1),
            (0, every, 3),
            (3, upper, 1),
            (1, lower, 3),
        )[which]
        view = self.view(part, phase, step, rows)
        return remote(
            view,
            view,
            self.send_sem.at[part, phase, which],
            self.recv_sem.at[part, phase, which],
            along(axis, way),
        )

    def start(self, phase):
        for part in range(2):
            for which in (0, 1):
                self.copy(part, phase, which).start()

    def pass_on(self, phase):
        for part in range(2):
            for which in (0, 1):
                self.copy(part, phase, which).wait_recv()
                self.copy(part, phase, which + 2).start()

    def finish(self, phase):
        for part in range(2):
            for which in (2, 3):
                self.copy(part, phase, which).wait_recv()

    def drain(self):
        for part in range(2):
            for phase in range(3):
                for which in range(4):
                    self.copy(part, phase, which).wait_send()


class Exchange:
    def __init__(self, src, first, second, dst, relay, send_sem, recv_sem, own_sem):
        self.bufs = (src, first, second, dst)
        self.relay = relay
        self.send_sem, self.recv_sem, self.own_sem = send_sem, recv_sem, own_sem

    def part(self, phase, buf, index, half):
        place = [slice(None)] * 3
        if half is not None:
            place[1 if phase == 0 else 0] = pl.ds(2 * half, 2)
        place[phase] = index
        return buf.at[tuple(place)]

    def own(self, phase):
        here = coordinates()[phase]
        return pltpu.make_async_copy(
            self.part(phase, self.bufs[phase], here, None),
            self.part(phase, self.bufs[phase + 1], here, None),
            self.own_sem.at[phase],
        )

    def copy(self, phase, which):
        here = coordinates()[phase]
        src, dst = self.bufs[phase], self.bufs[phase + 1]
        sems = (self.send_sem.at[phase, which], self.recv_sem.at[phase, which])
        if which < 2:
            step = (1, 3)[which]
            there = (here + step) % SIDE
            return remote(
                self.part(phase, src, there, None),
                self.part(phase, dst, here, None),
                *sems,
                along(phase, step),
            )
        half = which % 2
        step = (1, 3)[half]
        relay = self.relay.at[phase, half]
        if which < 4:
            there = (here + 2) % SIDE
            return remote(self.part(phase, src, there, half), relay, *sems, along(phase, step))
        origin = (here + 4 - step) % SIDE
        return remote(relay, self.part(phase, dst, origin, half), *sems, along(phase, step))

    def start(self, phase):
        self.own(phase).start()
        for which in (2, 3, 0, 1):
            self.copy(phase, which).start()

    def pass_on(self, phase):
        for which in (2, 3):
            self.copy(phase, which).wait_recv()
            self.copy(phase, which + 2).start()

    def finish(self, phase):
        self.own(phase).wait()
        for which in (0, 1, 4, 5):
            self.copy(phase, which).wait_recv()

    def drain(self):
        for phase in range(3):
            for which in range(6):
                self.copy(phase, which).wait_send()


def gather_kernel(split, src, buf, send_sem, recv_sem, own_sem):
    greet(())
    gather = Gather(src, buf, split, send_sem, recv_sem, own_sem)
    gather.own()
    for phase in range(3):
        gather.start(phase)
        gather.pass_on(phase)
        gather.finish(phase)
    gather.drain()


def gather_sems():
    return [
        pltpu.SemaphoreType.DMA((2, 3, 4)),
        pltpu.SemaphoreType.DMA((2, 3, 4)),
        pltpu.SemaphoreType.DMA((2,)),
    ]


VMEM_SPEC = pl.BlockSpec(memory_space=pltpu.VMEM)


def gather_tok(block, split, collective_id):
    rows = block.shape[1]
    return pl.pallas_call(
        functools.partial(gather_kernel, split),
        out_shape=jax.ShapeDtypeStruct((2, SIDE, SIDE, SIDE, rows, LANES), block.dtype),
        in_specs=[VMEM_SPEC],
        out_specs=VMEM_SPEC,
        scratch_shapes=gather_sems(),
        compiler_params=pltpu.CompilerParams(
            collective_id=collective_id, has_side_effects=True
        ),
        name="gather_tok",
    )(block)


def move_kernel(
    kv_src,
    out_src,
    cache_src,
    kv_buf,
    out_buf,
    cache_dst,
    first,
    second,
    relay,
    kv_send,
    kv_recv,
    kv_own,
    out_send,
    out_recv,
    out_own,
    cache_send,
    cache_recv,
    cache_own,
):
    greet(())
    kv = Gather(kv_src, kv_buf, HD, kv_send, kv_recv, kv_own)
    out = Gather(out_src, out_buf, 32, out_send, out_recv, out_own)
    cache = Exchange(cache_src, first, second, cache_dst, relay, cache_send, cache_recv, cache_own)
    kv.own()
    kv.start(0)
    out.own()
    kv.pass_on(0)
    kv.finish(0)
    kv.start(1)
    cache.start(0)
    kv.pass_on(1)
    kv.finish(1)
    kv.start(2)
    out.start(0)
    kv.pass_on(2)
    kv.finish(2)
    out.pass_on(0)
    cache.pass_on(0)
    out.finish(0)
    out.start(1)
    out.pass_on(1)
    out.finish(1)
    out.start(2)
    out.pass_on(2)
    out.finish(2)
    cache.finish(0)
    for phase in (1, 2):
        cache.start(phase)
        cache.pass_on(phase)
        cache.finish(phase)
    kv.drain()
    out.drain()
    cache.drain()


def move(kv_block, out_block, cache_block):
    def gathered(block):
        return jax.ShapeDtypeStruct((2, SIDE, SIDE, SIDE, block.shape[1], LANES), block.dtype)

    unit = cache_block.shape[3:]
    kind = cache_block.dtype
    return pl.pallas_call(
        move_kernel,
        out_shape=(
            gathered(kv_block),
            gathered(out_block),
            jax.ShapeDtypeStruct(cache_block.shape, kind),
        ),
        in_specs=[VMEM_SPEC] * 3,
        out_specs=[VMEM_SPEC] * 3,
        scratch_shapes=[
            pltpu.VMEM(cache_block.shape, kind),
            pltpu.VMEM(cache_block.shape, kind),
            pltpu.VMEM((3, 2, 2, SIDE, *unit), kind),
            *gather_sems(),
            *gather_sems(),
            pltpu.SemaphoreType.DMA((3, 6)),
            pltpu.SemaphoreType.DMA((3, 6)),
            pltpu.SemaphoreType.DMA((3,)),
        ],
        compiler_params=pltpu.CompilerParams(collective_id=1, has_side_effects=True),
        name="move",
    )(kv_block, out_block, cache_block)


def attend_group(group, masked, query, kv, top, total, weighted):
    z, y = group // SIDE, group % SIDE
    blocks = [(x, part) for x in range(SIDE) for part in range(2)]
    key = jnp.concatenate([kv[part, z, y, x, :HD, :] for x, part in blocks], axis=1)
    value = jnp.concatenate([kv[part, z, y, x, HD:, :] for x, part in blocks], axis=1)
    count = key.shape[1]
    width = query.shape[1] // QPK
    for head in range(QPK):
        cols = pl.ds(head * width, width)
        score = lax.dot_general(
            key, query[:, cols], (((0,), (0,)), ((), ())), preferred_element_type=jnp.float32
        )
        if masked:
            limit = coordinates()[2] * width
            rows = lax.broadcasted_iota(jnp.int32, (count, width), 0)
            lanes = lax.broadcasted_iota(jnp.int32, (count, width), 1)
            score = jnp.where(rows <= lanes + limit, score, LOWEST)
        before = top[:, cols]
        highest = jnp.maximum(before, jnp.max(score, axis=0, keepdims=True))
        expo = jnp.exp2((score - highest) * EXP2_SCALE)
        shrink = jnp.exp2((before - highest) * EXP2_SCALE)
        total[:, cols] = total[:, cols] * shrink + jnp.sum(expo, axis=0, keepdims=True)
        weighted[:, cols] = weighted[:, cols] * shrink + jnp.dot(
            value, expo.astype(jnp.bfloat16), preferred_element_type=jnp.float32
        )
        top[:, cols] = highest


def attend_kernel(query, kv, context, top, total, weighted):
    top[...] = jnp.full_like(top, LOWEST)
    total[...] = jnp.zeros_like(total)
    weighted[...] = jnp.zeros_like(weighted)
    last = lax.axis_index("tok") // SIDE

    def step(group, carry):
        attend_group(group, False, query, kv, top, total, weighted)
        return carry

    lax.fori_loop(0, last, step, 0)
    attend_group(last, True, query, kv, top, total, weighted)
    context[...] = (weighted[...] / total[...]).astype(context.dtype)


def attend(query, kv):
    columns = query.shape[1]
    return pl.pallas_call(
        attend_kernel,
        out_shape=jax.ShapeDtypeStruct((HD, columns), jnp.bfloat16),
        in_specs=[VMEM_SPEC] * 2,
        out_specs=VMEM_SPEC,
        scratch_shapes=[
            pltpu.VMEM((1, columns), jnp.float32),
            pltpu.VMEM((1, columns), jnp.float32),
            pltpu.VMEM((HD, columns), jnp.float32),
        ],
        name="attend",
    )(query, kv)


def pack_weight(block, lane_chunks, rows):
    height, width = block.shape
    block = jnp.pad(block, ((0, 0), (0, lane_chunks * LANES - width)))
    block = block.reshape(height, lane_chunks, LANES).transpose(1, 0, 2)
    block = block.reshape(lane_chunks * height, LANES)
    block = jnp.pad(block, ((0, 2 * rows - lane_chunks * height), (0, 0)))
    return block.reshape(2, rows, LANES)


def unpack_weight(buf, lane_chunks, height, width):
    rows = buf.shape[4]
    count = SIDE * SIDE * SIDE
    buf = buf.reshape(2, count, rows, LANES).transpose(1, 0, 2, 3)
    buf = buf.reshape(count, 2 * rows, LANES)[:, : lane_chunks * height]
    buf = buf.reshape(count, lane_chunks, height, LANES).transpose(0, 2, 1, 3)
    return buf.reshape(count * height, lane_chunks * LANES)[:, :width]


def project(hidden_in, norm_gain, weight):
    tok_rows = hidden_in.shape[0]
    float_rows = hidden_in.astype(jnp.float32)
    normed = (
        float_rows
        * lax.rsqrt(jnp.mean(float_rows * float_rows, axis=-1, keepdims=True) + NORM_EPS)
        * norm_gain
    ).astype(jnp.bfloat16)
    projected = lax.dot_general(
        weight, normed, (((0,), (1,)), ((), ())), preferred_element_type=jnp.float32
    ).reshape(QPK + 2, HD, tok_rows)
    half = HD // 2
    frequency = ROPE_BASE ** (-2.0 * jnp.arange(half, dtype=jnp.float32) / HD)
    positions = lax.axis_index("tok") * tok_rows + jnp.arange(tok_rows, dtype=jnp.int32)
    angles = frequency[:, None] * positions.astype(jnp.float32)[None, :]
    cosine, sines = jnp.cos(angles)[None], jnp.sin(angles)[None]
    front, back = projected[: QPK + 1, :half], projected[: QPK + 1, half:]
    turned = jnp.concatenate(
        [front * cosine - back * sines, back * cosine + front * sines], axis=1
    ).astype(jnp.bfloat16)
    query = turned[:QPK].transpose(1, 0, 2).reshape(HD, QPK * tok_rows)
    key_value = jnp.concatenate([turned[QPK], projected[QPK + 1].astype(jnp.bfloat16)], axis=0)
    key_value = key_value.reshape(2 * HD, 2, LANES).transpose(1, 0, 2)
    return query, key_value


def outgoing_blocks(prefill_cache, lengths, prefill_table, decode_table):
    tok_count = lax.axis_size("tok")
    my_index = lax.axis_index("tok")
    layers, slot_count, _, extent = prefill_cache.shape
    block_total = prefill_table.shape[0]
    per_request = block_total // lengths.shape[0]
    every_block = jnp.arange(block_total, dtype=jnp.int32)
    slots = jnp.arange(slot_count, dtype=jnp.int32)
    mine = prefill_table[:, None] == (my_index * slot_count + slots)[None, :]
    held_here = jnp.sum(jnp.where(mine, every_block[:, None], 0), axis=0)
    target = jnp.sum(jnp.where(mine, (decode_table // slot_count)[:, None], 0), axis=0)
    request = held_here // per_request
    requests = jnp.arange(lengths.shape[0], dtype=jnp.int32)
    request_len = jnp.sum(
        jnp.where(request[:, None] == requests[None, :], lengths[None, :], 0), axis=1
    )
    first_token = held_here % per_request * BLK
    live = first_token[:, None] + jnp.arange(BLK, dtype=jnp.int32)[None, :] < request_len[:, None]
    peers = jnp.arange(tok_count, dtype=jnp.int32)
    slot_of = jnp.sum(jnp.where(target[None, :] == peers[:, None], slots[None, :], 0), axis=1)
    origin = (my_index - (target - my_index)) % tok_count
    blocks = prefill_cache.reshape(layers, slot_count, BLK, extent // BLK)
    blocks = jnp.where(live[None, :, :, None], blocks, jnp.zeros_like(blocks))
    blocks = blocks.reshape(layers, slot_count, extent).transpose(1, 0, 2)
    blocks = jnp.take(blocks, slot_of, axis=0)
    blocks = blocks.reshape(SIDE, SIDE, SIDE, layers * extent // LANES, LANES)
    return blocks, origin


def on_device(
    hidden_in, norm_gain, w_qkv, w_out, prefill_cache, lengths, prefill_table, decode_table
):
    tok_rows = hidden_in.shape[0]
    layers, slot_count, kv_local, extent = prefill_cache.shape
    gathered = gather_tok(pack_weight(w_qkv, 4, 80), 48, 0)
    weight = unpack_weight(gathered, 4, *w_qkv.shape)
    query, key_value = project(hidden_in, norm_gain, weight)
    blocks, origin = outgoing_blocks(prefill_cache, lengths, prefill_table, decode_table)
    kv_all, out_all, arrived = move(key_value, pack_weight(w_out.T, 3, 64), blocks)
    context = attend(query, kv_all)
    context = context.reshape(HD, QPK, tok_rows).transpose(2, 1, 0).reshape(tok_rows, QPK * HD)
    out_weight = unpack_weight(out_all, 3, w_out.shape[1], w_out.shape[0])
    partial = lax.dot_general(
        context, out_weight, (((1,), (1,)), ((), ())), preferred_element_type=jnp.float32
    )
    attn_out = lax.psum_scatter(
        partial.astype(jnp.bfloat16), "head", scatter_dimension=1, tiled=True
    )
    arrived = arrived.reshape(slot_count, layers, extent)
    decode_cache = jnp.take(arrived, origin, axis=0).transpose(1, 0, 2)
    return attn_out, decode_cache.reshape(prefill_cache.shape)


def solution(mesh):
    in_specs = (
        P("tok", None),
        P(),
        P("tok", "head"),
        P("head", "tok"),
        P(None, "tok", "head", None),
        P(),
        P(),
        P(),
    )
    out_specs = (P("tok", "head"), P(None, "tok", "head", None))
    return jax.shard_map(
        on_device, mesh=mesh, in_specs=in_specs, out_specs=out_specs, check_vma=False
    )
```

```python
import functools
import math

import jax
import jax.numpy as jnp
from jax import lax
from jax.experimental import pallas as pl
from jax.experimental.pallas import tpu as pltpu
from jax.sharding import PartitionSpec as P

HD = 80
QPK = 4
BLK = 8
LANES = 128
SIDE = 4

NORM_EPS = 1e-05
ROPE_BASE = 1000000.0
LOWEST = -1e30
EXP2_SCALE = math.log2(math.e) / math.sqrt(HD)

MESH = pl.DeviceIdType.MESH


def coordinates():
    index = lax.axis_index("tok")
    return index // 16, (index // 4) % 4, index % 4


def along(axis, step):
    place = list(coordinates())
    place[axis] = (place[axis] + step) % SIDE
    return (place[0] * SIDE + place[1]) * SIDE + place[2]


def greet(far):
    barrier = pltpu.get_barrier_semaphore()
    peers = [along(axis, step) for axis in range(3) for step in (1, 3)]
    peers += [along(axis, 2) for axis in far]
    for peer in peers:
        pl.semaphore_signal(barrier, inc=1, device_id={"tok": peer}, device_id_type=MESH)
    pl.semaphore_wait(barrier, len(peers))


def remote(src, dst, send_sem, recv_sem, peer):
    return pltpu.make_async_remote_copy(
        src_ref=src,
        dst_ref=dst,
        send_sem=send_sem,
        recv_sem=recv_sem,
        device_id={"tok": peer},
        device_id_type=MESH,
    )


ORDERS = ((0, 1, 2), (0, 2, 1))


class Gather:
    def __init__(self, src, buf, split, send_sem, recv_sem, own_sem):
        self.src, self.buf, self.split = src, buf, split
        self.send_sem, self.recv_sem, self.own_sem = send_sem, recv_sem, own_sem
        self.sent = []

    def own(self):
        z, y, x = coordinates()
        for part in range(2):
            pltpu.make_async_copy(
                self.src.at[part], self.buf.at[part, z, y, x], self.own_sem.at[part]
            ).start()
        for part in range(2):
            pltpu.make_async_copy(
                self.src.at[part], self.buf.at[part, z, y, x], self.own_sem.at[part]
            ).wait()

    def view(self, part, phase, step, rows):
        done = ORDERS[part][:phase]
        axis = ORDERS[part][phase]
        place = list(coordinates())
        place[axis] = (place[axis] + step) % SIDE
        for seen in done:
            place[seen] = slice(None)
        return self.buf.at[(part, *place, rows, slice(None))]

    def copy(self, part, phase, which):
        axis = ORDERS[part][phase]
        every = slice(None)
        upper, lower = pl.ds(0, self.split), pl.ds(self.split, self.buf.shape[4] - self.split)
        step, rows, way = (
            (0, every, 1),
            (0, every, 3),
            (3, upper, 1),
            (1, lower, 3),
        )[which]
        view = self.view(part, phase, step, rows)
        return remote(
            view,
            view,
            self.send_sem.at[part, phase, which],
            self.recv_sem.at[part, phase, which],
            along(axis, way),
        )

    def start(self, phase):
        for part in range(2):
            for which in (0, 1):
                self.copy(part, phase, which).start()

    def pass_on(self, phase):
        for part in range(2):
            for which in (0, 1):
                self.copy(part, phase, which).wait_recv()
                self.copy(part, phase, which + 2).start()

    def finish(self, phase):
        for part in range(2):
            for which in (2, 3):
                self.copy(part, phase, which).wait_recv()

    def drain(self):
        for part in range(2):
            for phase in range(3):
                for which in range(4):
                    self.copy(part, phase, which).wait_send()


class Exchange:
    def __init__(self, order, phases, bufs, relay, send_sem, recv_sem, own_sem):
        self.order, self.phases, self.bufs, self.relay = order, phases, bufs, relay
        self.send_sem, self.recv_sem, self.own_sem = send_sem, recv_sem, own_sem

    def part(self, phase, buf, index, half):
        axis = self.order[phase]
        place = [slice(None)] * 3
        if half is not None:
            place[1 if axis == 0 else 0] = pl.ds(2 * half, 2)
        place[axis] = index
        return buf.at[tuple(place)]

    def own(self, phase):
        here = coordinates()[self.order[phase]]
        return pltpu.make_async_copy(
            self.part(phase, self.bufs[phase], here, None),
            self.part(phase, self.bufs[phase + 1], here, None),
            self.own_sem.at[phase],
        )

    def copy(self, phase, which):
        axis = self.order[phase]
        here = coordinates()[axis]
        src, dst = self.bufs[phase], self.bufs[phase + 1]
        sems = (self.send_sem.at[phase, which], self.recv_sem.at[phase, which])
        if which < 2:
            step = (1, 3)[which]
            there = (here + step) % SIDE
            return remote(
                self.part(phase, src, there, None),
                self.part(phase, dst, here, None),
                *sems,
                along(axis, step),
            )
        half = which % 2
        step = (1, 3)[half]
        relay = self.relay.at[phase - self.phases[0], half]
        if which < 4:
            there = (here + 2) % SIDE
            return remote(self.part(phase, src, there, half), relay, *sems, along(axis, step))
        origin = (here + 4 - step) % SIDE
        return remote(relay, self.part(phase, dst, origin, half), *sems, along(axis, step))

    def start(self, phase):
        self.own(phase).start()
        for which in (2, 3, 0, 1):
            self.copy(phase, which).start()

    def pass_on(self, phase):
        for which in (2, 3):
            self.copy(phase, which).wait_recv()
            self.copy(phase, which + 2).start()

    def finish(self, phase):
        self.own(phase).wait()
        for which in (0, 1, 4, 5):
            self.copy(phase, which).wait_recv()

    def drain(self):
        for phase in self.phases:
            for which in range(6):
                self.copy(phase, which).wait_send()


def relay_buffer(block, phases):
    return pltpu.VMEM((phases, 2, 2, SIDE, *block.shape[3:]), block.dtype)


def gather_kernel(
    split,
    src,
    cache_src,
    buf,
    cache_dst,
    relay,
    send_sem,
    recv_sem,
    own_sem,
    cache_send,
    cache_recv,
    cache_own,
):
    greet(())
    gather = Gather(src, buf, split, send_sem, recv_sem, own_sem)
    cache = Exchange(
        ORDERS[0], (0,), (cache_src, cache_dst), relay, cache_send, cache_recv, cache_own
    )
    gather.own()
    for phase in range(3):
        gather.start(phase)
        gather.pass_on(phase)
        if phase == 0:
            cache.start(0)
        gather.finish(phase)
    cache.pass_on(0)
    cache.finish(0)
    gather.drain()
    cache.drain()


def gather_sems():
    return [
        pltpu.SemaphoreType.DMA((2, 3, 4)),
        pltpu.SemaphoreType.DMA((2, 3, 4)),
        pltpu.SemaphoreType.DMA((2,)),
    ]


def exchange_sems():
    return [
        pltpu.SemaphoreType.DMA((3, 6)),
        pltpu.SemaphoreType.DMA((3, 6)),
        pltpu.SemaphoreType.DMA((3,)),
    ]


VMEM_SPEC = pl.BlockSpec(memory_space=pltpu.VMEM)


def like(block):
    return jax.ShapeDtypeStruct(block.shape, block.dtype)


def gathered(block):
    return jax.ShapeDtypeStruct((2, SIDE, SIDE, SIDE, block.shape[1], LANES), block.dtype)


def gather_tok(block, cache_block, split):
    return pl.pallas_call(
        functools.partial(gather_kernel, split),
        out_shape=(gathered(block), like(cache_block)),
        in_specs=[VMEM_SPEC] * 2,
        out_specs=[VMEM_SPEC] * 2,
        scratch_shapes=[relay_buffer(cache_block, 1), *gather_sems(), *exchange_sems()],
        compiler_params=pltpu.CompilerParams(collective_id=0, has_side_effects=True),
        name="gather_tok",
    )(block, cache_block)


def attend_group(z, k, masked, query, kv, top, total, weighted):
    my_z, my_y, my_x = coordinates()
    x, y = (my_x + k) % SIDE, (my_y + k) % SIDE
    places = [(0, other, x) for other in range(SIDE)] + [(1, y, other) for other in range(SIDE)]
    key = jnp.concatenate([kv[part, z, v, u, :HD, :] for part, v, u in places], axis=1)
    value = jnp.concatenate([kv[part, z, v, u, HD:, :] for part, v, u in places], axis=1)
    width = query.shape[1] // QPK
    if masked:
        shape = (LANES, width)
        ahead = lax.broadcasted_iota(jnp.int32, shape, 0) - lax.broadcasted_iota(
            jnp.int32, shape, 1
        )
        behind = [
            ((my_y - v) * SIDE + my_x - u) * width - part * LANES for part, v, u in places
        ]
    for head in range(QPK):
        cols = pl.ds(head * width, width)
        score = lax.dot_general(
            key, query[:, cols], (((0,), (0,)), ((), ())), preferred_element_type=jnp.float32
        )
        if masked:
            score = jnp.concatenate(
                [
                    jnp.where(
                        ahead <= limit, score[place * LANES : (place + 1) * LANES], LOWEST
                    )
                    for place, limit in enumerate(behind)
                ],
                axis=0,
            )
        before = top[:, cols]
        highest = jnp.maximum(before, jnp.max(score, axis=0, keepdims=True))
        expo = jnp.exp2((score - highest) * EXP2_SCALE)
        shrink = jnp.exp2((before - highest) * EXP2_SCALE)
        total[:, cols] = total[:, cols] * shrink + jnp.sum(expo, axis=0, keepdims=True)
        weighted[:, cols] = weighted[:, cols] * shrink + jnp.dot(
            value, expo.astype(jnp.bfloat16), preferred_element_type=jnp.float32
        )
        top[:, cols] = highest


def attend_kernel(
    query,
    kv_src,
    out_src,
    first_a,
    cache_b,
    context,
    out_buf,
    cache_dst_a,
    cache_dst_b,
    kv_buf,
    second_a,
    first_b,
    second_b,
    relay_a,
    relay_b,
    top,
    total,
    weighted,
    *sems,
):
    greet(())
    kv = Gather(kv_src, kv_buf, HD, *sems[0:3])
    out = Gather(out_src, out_buf, 32, *sems[3:6])
    half_a = Exchange(
        ORDERS[0], (1, 2), (None, first_a, second_a, cache_dst_a), relay_a, *sems[6:9]
    )
    half_b = Exchange(
        ORDERS[1], (0, 1, 2), (cache_b, first_b, second_b, cache_dst_b), relay_b, *sems[9:12]
    )
    my_z = coordinates()[0]

    def earlier_rows(k):
        def step(z, carry):
            attend_group(z, k, False, query, kv_buf, top, total, weighted)
            return carry

        lax.fori_loop(0, my_z, step, 0)

    def own_row(low, high):
        def step(k, carry):
            attend_group(my_z, k, True, query, kv_buf, top, total, weighted)
            return carry

        lax.fori_loop(low, high, step, 0)

    kv.own()
    kv.start(0)
    out.own()
    top[...] = jnp.full_like(top, LOWEST)
    total[...] = jnp.zeros_like(total)
    weighted[...] = jnp.zeros_like(weighted)
    kv.pass_on(0)
    half_b.start(0)
    kv.finish(0)
    kv.start(1)
    kv.pass_on(1)
    kv.finish(1)
    kv.start(2)
    out.start(0)
    own_row(0, 1)
    earlier_rows(0)
    kv.pass_on(2)
    out.pass_on(0)
    half_b.pass_on(0)
    earlier_rows(1)
    out.finish(0)
    out.start(1)
    half_b.finish(0)
    half_a.start(1)
    half_b.start(1)
    earlier_rows(3)
    kv.finish(2)
    half_a.pass_on(1)
    half_b.pass_on(1)
    out.pass_on(1)
    earlier_rows(2)
    half_a.finish(1)
    half_a.start(2)
    half_b.finish(1)
    half_b.start(2)
    out.finish(1)
    out.start(2)
    own_row(1, 4)
    half_a.pass_on(2)
    half_b.pass_on(2)
    out.pass_on(2)
    width = query.shape[1] // QPK
    for head in range(QPK):
        cols = pl.ds(head * width, width)
        context[pl.ds(head * HD, HD), :] = (weighted[:, cols] / total[:, cols]).astype(
            context.dtype
        )
    half_a.finish(2)
    half_b.finish(2)
    out.finish(2)
    kv.drain()
    out.drain()
    half_a.drain()
    half_b.drain()


def attend(query, kv_block, out_block, first_a, cache_b):
    columns = query.shape[1]
    cache = pltpu.VMEM(cache_b.shape, cache_b.dtype)
    return pl.pallas_call(
        attend_kernel,
        out_shape=(
            jax.ShapeDtypeStruct((QPK * HD, columns // QPK), jnp.bfloat16),
            gathered(out_block),
            like(first_a),
            like(cache_b),
        ),
        in_specs=[VMEM_SPEC] * 5,
        out_specs=[VMEM_SPEC] * 4,
        scratch_shapes=[
            pltpu.VMEM(gathered(kv_block).shape, kv_block.dtype),
            cache,
            cache,
            cache,
            relay_buffer(first_a, 2),
            relay_buffer(cache_b, 3),
            pltpu.VMEM((1, columns), jnp.float32),
            pltpu.VMEM((1, columns), jnp.float32),
            pltpu.VMEM((HD, columns), jnp.float32),
            *gather_sems(),
            *gather_sems(),
            *exchange_sems(),
            *exchange_sems(),
        ],
        compiler_params=pltpu.CompilerParams(collective_id=1, has_side_effects=True),
        name="attend",
    )(query, kv_block, out_block, first_a, cache_b)


def head_sum_kernel(part, result, swapped, pair, arrived, swap_sem, send_sem, recv_sem):
    index = lax.axis_index("head")
    chip, core = index // 2, index % 2
    partner = chip * 2 + 1 - core
    others = [((chip + step) % SIDE) * 2 + core for step in (1, 2, 3)]
    barrier = pltpu.get_barrier_semaphore()
    for peer in (partner, *others):
        pl.semaphore_signal(barrier, inc=1, device_id={"head": peer}, device_id_type=MESH)
    pl.semaphore_wait(barrier, 4)

    def to_partner(step):
        return pltpu.make_async_remote_copy(
            src_ref=part.at[(chip + step) % SIDE, 1 - core],
            dst_ref=swapped.at[step],
            send_sem=swap_sem.at[0, step],
            recv_sem=swap_sem.at[1, step],
            device_id={"head": partner},
            device_id_type=MESH,
        )

    def to_chip(step):
        return pltpu.make_async_remote_copy(
            src_ref=pair.at[step],
            dst_ref=arrived.at[step],
            send_sem=send_sem.at[step],
            recv_sem=recv_sem.at[step],
            device_id={"head": others[step - 1]},
            device_id_type=MESH,
        )

    def add(step):
        mine = part[(chip + step) % SIDE, core].astype(jnp.float32)
        return mine + swapped[step].astype(jnp.float32)

    order = (2, 1, 3)
    for step in (*order, 0):
        to_partner(step).start()
    for place, step in enumerate(order):
        to_partner(step).wait_recv()
        pair[step] = add(step).astype(pair.dtype)
        if place:
            to_chip(order[place - 1]).start()
    to_partner(0).wait_recv()
    pair[0] = add(0).astype(pair.dtype)
    to_chip(order[-1]).start()
    whole = pair[0].astype(jnp.float32)
    for step in (1, 3, 2):
        to_chip(step).wait_recv()
        whole = whole + arrived[step].astype(jnp.float32)
    result[...] = whole.astype(result.dtype)
    for step in order:
        to_chip(step).wait_send()
    for step in range(SIDE):
        to_partner(step).wait_send()


def head_sum(part):
    slices = pltpu.VMEM((SIDE, *part.shape[2:]), part.dtype)
    return pl.pallas_call(
        head_sum_kernel,
        out_shape=jax.ShapeDtypeStruct(part.shape[2:], part.dtype),
        in_specs=[VMEM_SPEC],
        out_specs=VMEM_SPEC,
        scratch_shapes=[
            slices,
            slices,
            slices,
            pltpu.SemaphoreType.DMA((2, SIDE)),
            pltpu.SemaphoreType.DMA((SIDE,)),
            pltpu.SemaphoreType.DMA((SIDE,)),
        ],
        compiler_params=pltpu.CompilerParams(collective_id=2, has_side_effects=True),
        name="head_sum",
    )(part)


def pack_weight(block, lane_chunks, rows):
    height, width = block.shape
    block = jnp.pad(block, ((0, 0), (0, lane_chunks * LANES - width)))
    block = block.reshape(height, lane_chunks, LANES).transpose(1, 0, 2)
    block = block.reshape(lane_chunks * height, LANES)
    block = jnp.pad(block, ((0, 2 * rows - lane_chunks * height), (0, 0)))
    return block.reshape(2, rows, LANES)


def unpack_weight(buf, lane_chunks, height, width):
    rows = buf.shape[4]
    count = SIDE * SIDE * SIDE
    buf = buf.reshape(2, count, rows, LANES).transpose(1, 0, 2, 3)
    buf = buf.reshape(count, 2 * rows, LANES)[:, : lane_chunks * height]
    buf = buf.reshape(count, lane_chunks, height, LANES).transpose(0, 2, 1, 3)
    return buf.reshape(count * height, lane_chunks * LANES)[:, :width]


def project(hidden_in, norm_gain, weight):
    tok_rows = hidden_in.shape[0]
    float_rows = hidden_in.astype(jnp.float32)
    normed = (
        float_rows
        * lax.rsqrt(jnp.mean(float_rows * float_rows, axis=-1, keepdims=True) + NORM_EPS)
        * norm_gain
    ).astype(jnp.bfloat16)
    projected = lax.dot_general(
        weight, normed, (((0,), (1,)), ((), ())), preferred_element_type=jnp.float32
    ).reshape(QPK + 2, HD, tok_rows)
    half = HD // 2
    frequency = ROPE_BASE ** (-2.0 * jnp.arange(half, dtype=jnp.float32) / HD)
    positions = lax.axis_index("tok") * tok_rows + jnp.arange(tok_rows, dtype=jnp.int32)
    angles = frequency[:, None] * positions.astype(jnp.float32)[None, :]
    cosine, sines = jnp.cos(angles)[None], jnp.sin(angles)[None]
    front, back = projected[: QPK + 1, :half], projected[: QPK + 1, half:]
    turned = jnp.concatenate(
        [front * cosine - back * sines, back * cosine + front * sines], axis=1
    ).astype(jnp.bfloat16)
    query = turned[:QPK].transpose(1, 0, 2).reshape(HD, QPK * tok_rows)
    key_value = jnp.concatenate([turned[QPK], projected[QPK + 1].astype(jnp.bfloat16)], axis=0)
    key_value = key_value.reshape(2 * HD, 2, LANES).transpose(1, 0, 2)
    return query, key_value


def outgoing_blocks(prefill_cache, lengths, prefill_table, decode_table):
    tok_count = lax.axis_size("tok")
    my_index = lax.axis_index("tok")
    layers, slot_count, _, extent = prefill_cache.shape
    block_total = prefill_table.shape[0]
    per_request = block_total // lengths.shape[0]
    every_block = jnp.arange(block_total, dtype=jnp.int32)
    slots = jnp.arange(slot_count, dtype=jnp.int32)
    mine = prefill_table[:, None] == (my_index * slot_count + slots)[None, :]
    held_here = jnp.sum(jnp.where(mine, every_block[:, None], 0), axis=0)
    target = jnp.sum(jnp.where(mine, (decode_table // slot_count)[:, None], 0), axis=0)
    request = held_here // per_request
    requests = jnp.arange(lengths.shape[0], dtype=jnp.int32)
    request_len = jnp.sum(
        jnp.where(request[:, None] == requests[None, :], lengths[None, :], 0), axis=1
    )
    first_token = held_here % per_request * BLK
    live = first_token[:, None] + jnp.arange(BLK, dtype=jnp.int32)[None, :] < request_len[:, None]
    peers = jnp.arange(tok_count, dtype=jnp.int32)
    slot_of = jnp.sum(jnp.where(target[None, :] == peers[:, None], slots[None, :], 0), axis=1)
    origin = (my_index - (target - my_index)) % tok_count
    blocks = prefill_cache.reshape(layers, slot_count, BLK, extent // BLK)
    blocks = jnp.where(live[None, :, :, None], blocks, jnp.zeros_like(blocks))
    blocks = blocks.reshape(layers, slot_count, extent).transpose(1, 0, 2)
    blocks = jnp.take(blocks, slot_of, axis=0)
    near = layers // 2
    halves = [
        half.reshape(SIDE, SIDE, SIDE, near * extent // LANES, LANES)
        for half in (blocks[:, :near], blocks[:, near:])
    ]
    return halves, origin


def on_device(
    hidden_in, norm_gain, w_qkv, w_out, prefill_cache, lengths, prefill_table, decode_table
):
    layers, slot_count, kv_local, extent = prefill_cache.shape
    (cache_a, cache_b), origin = outgoing_blocks(
        prefill_cache, lengths, prefill_table, decode_table
    )
    weights, first_a = gather_tok(pack_weight(w_qkv, 4, 80), cache_a, 48)
    query, key_value = project(hidden_in, norm_gain, unpack_weight(weights, 4, *w_qkv.shape))
    context, out_all, *arrived = attend(
        query, key_value, pack_weight(w_out.T, 3, 64), first_a, cache_b
    )
    out_weight = unpack_weight(out_all, 3, w_out.shape[1], w_out.shape[0])
    part = jnp.dot(out_weight, context, preferred_element_type=jnp.float32).astype(jnp.bfloat16)
    heads = lax.axis_size("head")
    part = part.reshape(heads // 2, 2, part.shape[0] // heads, part.shape[1])
    attn_out = head_sum(part).T
    arrived = jnp.concatenate(
        [half.reshape(slot_count, layers // 2, extent) for half in arrived], axis=1
    )
    decode_cache = jnp.take(arrived, origin, axis=0).transpose(1, 0, 2)
    return attn_out, decode_cache.reshape(prefill_cache.shape)


def solution(mesh):
    in_specs = (
        P("tok", None),
        P(),
        P("tok", "head"),
        P("head", "tok"),
        P(None, "tok", "head", None),
        P(),
        P(),
        P(),
    )
    out_specs = (P("tok", "head"), P(None, "tok", "head", None))
    return jax.shard_map(
        on_device, mesh=mesh, in_specs=in_specs, out_specs=out_specs, check_vma=False
    )
```

```python
import functools
import math

import jax
import jax.numpy as jnp
from jax import lax
from jax.experimental import pallas as pl
from jax.experimental.pallas import tpu as pltpu
from jax.sharding import PartitionSpec as P

HD = 80
QPK = 4
BLK = 8
LANES = 128
NEAR = 3 * LANES
SIDE = 4

NORM_EPS = 1e-05
ROPE_BASE = 1000000.0
LOWEST = -1e30
EXP2_SCALE = math.log2(math.e) / math.sqrt(HD)

MESH = pl.DeviceIdType.MESH


def coordinates():
    index = lax.axis_index("tok")
    return index // 16, (index // 4) % 4, index % 4


def along(axis, step):
    place = list(coordinates())
    place[axis] = (place[axis] + step) % SIDE
    return (place[0] * SIDE + place[1]) * SIDE + place[2]


def greet(far):
    barrier = pltpu.get_barrier_semaphore()
    peers = [along(axis, step) for axis in range(3) for step in (1, 3)]
    peers += [along(axis, 2) for axis in far]
    for peer in peers:
        pl.semaphore_signal(barrier, inc=1, device_id={"tok": peer}, device_id_type=MESH)
    pl.semaphore_wait(barrier, len(peers))


def remote(src, dst, send_sem, recv_sem, peer):
    return pltpu.make_async_remote_copy(
        src_ref=src,
        dst_ref=dst,
        send_sem=send_sem,
        recv_sem=recv_sem,
        device_id={"tok": peer},
        device_id_type=MESH,
    )


ORDERS = ((0, 1, 2), (0, 2, 1))


class Gather:
    def __init__(self, src, buf, split, send_sem, recv_sem, own_sem):
        self.src, self.buf, self.split = src, buf, split
        self.send_sem, self.recv_sem, self.own_sem = send_sem, recv_sem, own_sem
        self.sent = []

    def own(self):
        z, y, x = coordinates()
        for part in range(2):
            pltpu.make_async_copy(
                self.src.at[part], self.buf.at[part, z, y, x], self.own_sem.at[part]
            ).start()
        for part in range(2):
            pltpu.make_async_copy(
                self.src.at[part], self.buf.at[part, z, y, x], self.own_sem.at[part]
            ).wait()

    def view(self, part, phase, step, rows):
        done = ORDERS[part][:phase]
        axis = ORDERS[part][phase]
        place = list(coordinates())
        place[axis] = (place[axis] + step) % SIDE
        for seen in done:
            place[seen] = slice(None)
        return self.buf.at[(part, *place, rows, slice(None))]

    def copy(self, part, phase, which):
        axis = ORDERS[part][phase]
        every = slice(None)
        upper, lower = pl.ds(0, self.split), pl.ds(self.split, self.buf.shape[4] - self.split)
        step, rows, way = (
            (0, every, 1),
            (0, every, 3),
            (3, upper, 1),
            (1, lower, 3),
        )[which]
        view = self.view(part, phase, step, rows)
        return remote(
            view,
            view,
            self.send_sem.at[part, phase, which],
            self.recv_sem.at[part, phase, which],
            along(axis, way),
        )

    def start(self, phase):
        for part in range(2):
            for which in (0, 1):
                self.copy(part, phase, which).start()

    def pass_on(self, phase):
        for part in range(2):
            for which in (0, 1):
                self.copy(part, phase, which).wait_recv()
                self.copy(part, phase, which + 2).start()

    def finish(self, phase):
        for part in range(2):
            for which in (2, 3):
                self.copy(part, phase, which).wait_recv()

    def drain(self):
        for part in range(2):
            for phase in range(3):
                for which in range(4):
                    self.copy(part, phase, which).wait_send()


class Flow:
    def __init__(self, src, buf, split, z_send, z_recv, send_sem, recv_sem, own_sem):
        self.src, self.buf, self.split = src, buf, split
        self.z_send, self.z_recv = z_send, z_recv
        self.send_sem, self.recv_sem, self.own_sem = send_sem, recv_sem, own_sem

    def own(self):
        z, y, x = coordinates()
        copy = pltpu.make_async_copy(self.src, self.buf.at[:, z, y, x], self.own_sem)
        copy.start()
        copy.wait()

    def plan(self, which):
        upper, lower = pl.ds(0, self.split), pl.ds(self.split, self.buf.shape[4] - self.split)
        every = slice(None)
        return ((0, every, 1), (0, every, 3), (3, upper, 1), (1, lower, 3))[which]

    def z_copy(self, which):
        step, rows, way = self.plan(which)
        z, y, x = coordinates()
        view = self.buf.at[:, (z + step) % SIDE, y, x, rows, :]
        return remote(view, view, self.z_send.at[which], self.z_recv.at[which], along(0, way))

    def z_start(self):
        self.z_copy(0).start()
        self.z_copy(1).start()

    def z_pass_on(self):
        for which in (0, 1):
            self.z_copy(which).wait_recv()
            self.z_copy(which + 2).start()

    def z_finish(self):
        for which in (2, 3):
            self.z_copy(which).wait_recv()

    def copy(self, row, part, phase, which):
        step, rows, way = self.plan(which)
        axis = ORDERS[part][1 + phase]
        place = list(coordinates())
        place[0] = (place[0] + row) % SIDE
        place[axis] = (place[axis] + step) % SIDE
        if phase:
            place[ORDERS[part][1]] = slice(None)
        view = self.buf.at[(part, *place, rows, slice(None))]
        sem = (row, part, phase, which)
        return remote(view, view, self.send_sem.at[sem], self.recv_sem.at[sem], along(axis, way))

    def start(self, row, phase):
        for part in range(2):
            for which in (0, 1):
                self.copy(row, part, phase, which).start()

    def pass_on(self, row, phase):
        for part in range(2):
            for which in (0, 1):
                self.copy(row, part, phase, which).wait_recv()
                self.copy(row, part, phase, which + 2).start()

    def finish(self, row, phase):
        for part in range(2):
            for which in (2, 3):
                self.copy(row, part, phase, which).wait_recv()

    def drain(self):
        for which in range(4):
            self.z_copy(which).wait_send()
        for row in range(SIDE):
            for part in range(2):
                for phase in range(2):
                    for which in range(4):
                        self.copy(row, part, phase, which).wait_send()

    def head(self, beside):
        self.own()
        self.z_start()
        self.start(0, 0)
        self.pass_on(0, 0)
        self.finish(0, 0)
        self.start(0, 1)
        self.z_pass_on()
        beside()
        self.start(3, 0)
        self.start(1, 0)
        self.pass_on(0, 1)
        for row in (3, 1):
            self.pass_on(row, 0)
        for row in (3, 1):
            self.finish(row, 0)
            self.start(row, 1)
        self.finish(0, 1)


class Exchange:
    def __init__(self, order, phases, bufs, relay, send_sem, recv_sem, own_sem):
        self.order, self.phases, self.bufs, self.relay = order, phases, bufs, relay
        self.send_sem, self.recv_sem, self.own_sem = send_sem, recv_sem, own_sem

    def part(self, phase, buf, index, half):
        axis = self.order[phase]
        place = [slice(None)] * 3
        if half is not None:
            place[1 if axis == 0 else 0] = pl.ds(2 * half, 2)
        place[axis] = index
        return buf.at[tuple(place)]

    def own(self, phase):
        here = coordinates()[self.order[phase]]
        return pltpu.make_async_copy(
            self.part(phase, self.bufs[phase], here, None),
            self.part(phase, self.bufs[phase + 1], here, None),
            self.own_sem.at[phase],
        )

    def copy(self, phase, which):
        axis = self.order[phase]
        here = coordinates()[axis]
        src, dst = self.bufs[phase], self.bufs[phase + 1]
        sems = (self.send_sem.at[phase, which], self.recv_sem.at[phase, which])
        if which < 2:
            step = (1, 3)[which]
            there = (here + step) % SIDE
            return remote(
                self.part(phase, src, there, None),
                self.part(phase, dst, here, None),
                *sems,
                along(axis, step),
            )
        half = which % 2
        step = (1, 3)[half]
        relay = self.relay.at[phase - self.phases[0], half]
        if which < 4:
            there = (here + 2) % SIDE
            return remote(self.part(phase, src, there, half), relay, *sems, along(axis, step))
        origin = (here + 4 - step) % SIDE
        return remote(relay, self.part(phase, dst, origin, half), *sems, along(axis, step))

    def start(self, phase):
        self.own(phase).start()
        for which in (2, 3, 0, 1):
            self.copy(phase, which).start()

    def pass_on(self, phase):
        for which in (2, 3):
            self.copy(phase, which).wait_recv()
            self.copy(phase, which + 2).start()

    def finish(self, phase):
        self.own(phase).wait()
        for which in (0, 1, 4, 5):
            self.copy(phase, which).wait_recv()

    def drain(self):
        for phase in self.phases:
            for which in range(6):
                self.copy(phase, which).wait_send()


def relay_buffer(block, phases):
    return pltpu.VMEM((phases, 2, 2, SIDE, *block.shape[3:]), block.dtype)


def gather_kernel(split, src, cache_src, buf, cache_dst, relay, *sems):
    greet(())
    gather = Flow(src, buf, split, *sems[0:5])
    cache = Exchange(ORDERS[0], (0,), (cache_src, cache_dst), relay, *sems[5:8])
    gather.head(lambda: cache.start(0))
    gather.z_finish()
    gather.start(2, 0)
    for row in (3, 1):
        gather.pass_on(row, 1)
    gather.pass_on(2, 0)
    gather.finish(2, 0)
    gather.start(2, 1)
    for row in (3, 1):
        gather.finish(row, 1)
    gather.pass_on(2, 1)
    cache.pass_on(0)
    gather.finish(2, 1)
    cache.finish(0)
    gather.drain()
    cache.drain()


def flow_sems():
    return [
        pltpu.SemaphoreType.DMA((4,)),
        pltpu.SemaphoreType.DMA((4,)),
        pltpu.SemaphoreType.DMA((SIDE, 2, 2, 4)),
        pltpu.SemaphoreType.DMA((SIDE, 2, 2, 4)),
        pltpu.SemaphoreType.DMA,
    ]


def gather_sems():
    return [
        pltpu.SemaphoreType.DMA((2, 3, 4)),
        pltpu.SemaphoreType.DMA((2, 3, 4)),
        pltpu.SemaphoreType.DMA((2,)),
    ]


def exchange_sems():
    return [
        pltpu.SemaphoreType.DMA((3, 6)),
        pltpu.SemaphoreType.DMA((3, 6)),
        pltpu.SemaphoreType.DMA((3,)),
    ]


VMEM_SPEC = pl.BlockSpec(memory_space=pltpu.VMEM)


def like(block):
    return jax.ShapeDtypeStruct(block.shape, block.dtype)


def gathered(block):
    return jax.ShapeDtypeStruct((2, SIDE, SIDE, SIDE, block.shape[1], LANES), block.dtype)


def gather_tok(block, cache_block, split):
    return pl.pallas_call(
        functools.partial(gather_kernel, split),
        out_shape=(gathered(block), like(cache_block)),
        in_specs=[VMEM_SPEC] * 2,
        out_specs=[VMEM_SPEC] * 2,
        scratch_shapes=[relay_buffer(cache_block, 1), *flow_sems(), *exchange_sems()],
        compiler_params=pltpu.CompilerParams(collective_id=0, has_side_effects=True),
        name="gather_tok",
    )(block, cache_block)


def attend_group(z, y, masked, query, kv, top, total, weighted):
    places = [(part, x) for x in range(SIDE) for part in range(2)]
    key = jnp.concatenate([kv[part, z, y, x, :HD, :] for part, x in places], axis=1)
    value = jnp.concatenate([kv[part, z, y, x, HD:, :] for part, x in places], axis=1)
    width = query.shape[1] // QPK
    if masked:
        shape = (LANES, width)
        ahead = lax.broadcasted_iota(jnp.int32, shape, 0) - lax.broadcasted_iota(
            jnp.int32, shape, 1
        )
        my_x = coordinates()[2]
        behind = [(my_x - x) * width - part * LANES for part, x in places]
    for head in range(QPK):
        cols = pl.ds(head * width, width)
        score = lax.dot_general(
            key, query[:, cols], (((0,), (0,)), ((), ())), preferred_element_type=jnp.float32
        )
        if masked:
            score = jnp.concatenate(
                [
                    jnp.where(
                        ahead <= limit, score[place * LANES : (place + 1) * LANES], LOWEST
                    )
                    for place, limit in enumerate(behind)
                ],
                axis=0,
            )
        before = top[:, cols]
        highest = jnp.maximum(before, jnp.max(score, axis=0, keepdims=True))
        expo = jnp.exp2((score - highest) * EXP2_SCALE)
        shrink = jnp.exp2((before - highest) * EXP2_SCALE)
        total[:, cols] = total[:, cols] * shrink + jnp.sum(expo, axis=0, keepdims=True)
        weighted[:, cols] = weighted[:, cols] * shrink + jnp.dot(
            value, expo.astype(jnp.bfloat16), preferred_element_type=jnp.float32
        )
        top[:, cols] = highest


def attend_kernel(
    query,
    kv_src,
    out_src,
    first_a,
    cache_b,
    context,
    out_buf,
    cache_dst_a,
    cache_dst_b,
    kv_buf,
    second_a,
    first_b,
    second_b,
    relay_a,
    relay_b,
    top,
    total,
    weighted,
    *sems,
):
    greet(())
    kv = Flow(kv_src, kv_buf, HD, *sems[0:5])
    out = Gather(out_src, out_buf, 32, *sems[5:8])
    half_a = Exchange(
        ORDERS[0], (1, 2), (None, first_a, second_a, cache_dst_a), relay_a, *sems[8:11]
    )
    half_b = Exchange(
        ORDERS[1], (0, 1, 2), (cache_b, first_b, second_b, cache_dst_b), relay_b, *sems[11:14]
    )
    my_z, my_y, _ = coordinates()
    state = (query, kv_buf, top, total, weighted)

    def groups(z, low, count):
        def step(y, carry):
            attend_group(z, y, False, *state)
            return carry

        lax.fori_loop(low, low + count, step, 0)

    def row(step, half):
        earlier = my_z // (SIDE - step)
        earlier = jnp.minimum(earlier, 1)
        groups((my_z + step) % SIDE, 2 * half, 2 * earlier)

    top[...] = jnp.full_like(top, LOWEST)
    total[...] = jnp.zeros_like(total)
    weighted[...] = jnp.zeros_like(weighted)
    kv.head(lambda: half_b.start(0))
    out.own()
    attend_group(my_z, my_y, True, *state)
    kv.z_finish()
    kv.start(2, 0)
    out.start(0)
    groups(my_z, 0, my_y)
    for way in (3, 1):
        kv.pass_on(way, 1)
    kv.pass_on(2, 0)
    kv.finish(2, 0)
    kv.start(2, 1)
    half_a.start(1)
    out.pass_on(0)
    kv.finish(3, 1)
    row(3, 0)
    kv.pass_on(2, 1)
    half_b.pass_on(0)
    half_a.pass_on(1)
    out.finish(0)
    out.start(1)
    row(3, 1)
    kv.finish(1, 1)
    kv.finish(2, 1)
    out.pass_on(1)
    half_a.finish(1)
    half_a.start(2)
    row(1, 0)
    half_b.finish(0)
    half_b.start(1)
    half_a.pass_on(2)
    out.finish(1)
    out.start(2)
    row(1, 1)
    half_b.pass_on(1)
    out.pass_on(2)
    row(2, 0)
    half_b.finish(1)
    half_b.start(2)
    row(2, 1)
    half_b.pass_on(2)
    width = query.shape[1] // QPK
    for head in range(QPK):
        cols = pl.ds(head * width, width)
        context[pl.ds(head * HD, HD), :] = (weighted[:, cols] / total[:, cols]).astype(
            context.dtype
        )
    half_a.finish(2)
    half_b.finish(2)
    out.finish(2)
    kv.drain()
    out.drain()
    half_a.drain()
    half_b.drain()


def attend(query, kv_block, out_block, first_a, cache_b):
    columns = query.shape[1]
    cache = pltpu.VMEM(cache_b.shape, cache_b.dtype)
    return pl.pallas_call(
        attend_kernel,
        out_shape=(
            jax.ShapeDtypeStruct((QPK * HD, columns // QPK), jnp.bfloat16),
            gathered(out_block),
            like(first_a),
            like(cache_b),
        ),
        in_specs=[VMEM_SPEC] * 5,
        out_specs=[VMEM_SPEC] * 4,
        scratch_shapes=[
            pltpu.VMEM(gathered(kv_block).shape, kv_block.dtype),
            pltpu.VMEM(first_a.shape, first_a.dtype),
            cache,
            cache,
            relay_buffer(first_a, 2),
            relay_buffer(cache_b, 3),
            pltpu.VMEM((1, columns), jnp.float32),
            pltpu.VMEM((1, columns), jnp.float32),
            pltpu.VMEM((HD, columns), jnp.float32),
            *flow_sems(),
            *gather_sems(),
            *exchange_sems(),
            *exchange_sems(),
        ],
        compiler_params=pltpu.CompilerParams(collective_id=1, has_side_effects=True),
        name="attend",
    )(query, kv_block, out_block, first_a, cache_b)


def head_sum_kernel(part, result, swapped, pair, arrived, swap_sem, send_sem, recv_sem):
    index = lax.axis_index("head")
    chip, core = index // 2, index % 2
    partner = chip * 2 + 1 - core
    others = [((chip + step) % SIDE) * 2 + core for step in (1, 2, 3)]
    barrier = pltpu.get_barrier_semaphore()
    for peer in (partner, *others):
        pl.semaphore_signal(barrier, inc=1, device_id={"head": peer}, device_id_type=MESH)
    pl.semaphore_wait(barrier, 4)

    def to_partner(step):
        return pltpu.make_async_remote_copy(
            src_ref=part.at[(chip + step) % SIDE, 1 - core],
            dst_ref=swapped.at[step],
            send_sem=swap_sem.at[0, step],
            recv_sem=swap_sem.at[1, step],
            device_id={"head": partner},
            device_id_type=MESH,
        )

    def to_chip(step):
        return pltpu.make_async_remote_copy(
            src_ref=pair.at[step],
            dst_ref=arrived.at[step],
            send_sem=send_sem.at[step],
            recv_sem=recv_sem.at[step],
            device_id={"head": others[step - 1]},
            device_id_type=MESH,
        )

    def add(step):
        mine = part[(chip + step) % SIDE, core].astype(jnp.float32)
        return mine + swapped[step].astype(jnp.float32)

    order = (2, 1, 3)
    for step in (*order, 0):
        to_partner(step).start()
    for place, step in enumerate(order):
        to_partner(step).wait_recv()
        pair[step] = add(step).astype(pair.dtype)
        if place:
            to_chip(order[place - 1]).start()
    to_partner(0).wait_recv()
    pair[0] = add(0).astype(pair.dtype)
    to_chip(order[-1]).start()
    whole = pair[0].astype(jnp.float32)
    for step in (1, 3, 2):
        to_chip(step).wait_recv()
        whole = whole + arrived[step].astype(jnp.float32)
    result[...] = whole.astype(result.dtype)
    for step in order:
        to_chip(step).wait_send()
    for step in range(SIDE):
        to_partner(step).wait_send()


def head_sum(part):
    slices = pltpu.VMEM((SIDE, *part.shape[2:]), part.dtype)
    return pl.pallas_call(
        head_sum_kernel,
        out_shape=jax.ShapeDtypeStruct(part.shape[2:], part.dtype),
        in_specs=[VMEM_SPEC],
        out_specs=VMEM_SPEC,
        scratch_shapes=[
            slices,
            slices,
            slices,
            pltpu.SemaphoreType.DMA((2, SIDE)),
            pltpu.SemaphoreType.DMA((SIDE,)),
            pltpu.SemaphoreType.DMA((SIDE,)),
        ],
        compiler_params=pltpu.CompilerParams(collective_id=2, has_side_effects=True),
        name="head_sum",
    )(part)


def pack_weight(block, lane_chunks, rows):
    height, width = block.shape
    block = jnp.pad(block, ((0, 0), (0, lane_chunks * LANES - width)))
    block = block.reshape(height, lane_chunks, LANES).transpose(1, 0, 2)
    block = block.reshape(lane_chunks * height, LANES)
    block = jnp.pad(block, ((0, 2 * rows - lane_chunks * height), (0, 0)))
    return block.reshape(2, rows, LANES)


def unpack_weight(buf, lane_chunks, height, width):
    rows = buf.shape[4]
    count = SIDE * SIDE * SIDE
    buf = buf.reshape(2, count, rows, LANES).transpose(1, 0, 2, 3)
    buf = buf.reshape(count, 2 * rows, LANES)[:, : lane_chunks * height]
    buf = buf.reshape(count, lane_chunks, height, LANES).transpose(0, 2, 1, 3)
    return buf.reshape(count * height, lane_chunks * LANES)[:, :width]


def project(hidden_in, norm_gain, weight):
    tok_rows = hidden_in.shape[0]
    float_rows = hidden_in.astype(jnp.float32)
    normed = (
        float_rows
        * lax.rsqrt(jnp.mean(float_rows * float_rows, axis=-1, keepdims=True) + NORM_EPS)
        * norm_gain
    ).astype(jnp.bfloat16)
    projected = lax.dot_general(
        weight, normed, (((0,), (1,)), ((), ())), preferred_element_type=jnp.float32
    ).reshape(QPK + 2, HD, tok_rows)
    half = HD // 2
    frequency = ROPE_BASE ** (-2.0 * jnp.arange(half, dtype=jnp.float32) / HD)
    positions = lax.axis_index("tok") * tok_rows + jnp.arange(tok_rows, dtype=jnp.int32)
    angles = frequency[:, None] * positions.astype(jnp.float32)[None, :]
    cosine, sines = jnp.cos(angles)[None], jnp.sin(angles)[None]
    front, back = projected[: QPK + 1, :half], projected[: QPK + 1, half:]
    turned = jnp.concatenate(
        [front * cosine - back * sines, back * cosine + front * sines], axis=1
    ).astype(jnp.bfloat16)
    query = turned[:QPK].transpose(1, 0, 2).reshape(HD, QPK * tok_rows)
    key_value = jnp.concatenate([turned[QPK], projected[QPK + 1].astype(jnp.bfloat16)], axis=0)
    key_value = key_value.reshape(2 * HD, 2, LANES).transpose(1, 0, 2)
    return query, key_value


def outgoing_blocks(prefill_cache, lengths, prefill_table, decode_table):
    tok_count = lax.axis_size("tok")
    my_index = lax.axis_index("tok")
    layers, slot_count, _, extent = prefill_cache.shape
    block_total = prefill_table.shape[0]
    per_request = block_total // lengths.shape[0]
    every_block = jnp.arange(block_total, dtype=jnp.int32)
    slots = jnp.arange(slot_count, dtype=jnp.int32)
    mine = prefill_table[:, None] == (my_index * slot_count + slots)[None, :]
    held_here = jnp.sum(jnp.where(mine, every_block[:, None], 0), axis=0)
    target = jnp.sum(jnp.where(mine, (decode_table // slot_count)[:, None], 0), axis=0)
    request = held_here // per_request
    requests = jnp.arange(lengths.shape[0], dtype=jnp.int32)
    request_len = jnp.sum(
        jnp.where(request[:, None] == requests[None, :], lengths[None, :], 0), axis=1
    )
    first_token = held_here % per_request * BLK
    live = first_token[:, None] + jnp.arange(BLK, dtype=jnp.int32)[None, :] < request_len[:, None]
    peers = jnp.arange(tok_count, dtype=jnp.int32)
    slot_of = jnp.sum(jnp.where(target[None, :] == peers[:, None], slots[None, :], 0), axis=1)
    origin = (my_index - (target - my_index)) % tok_count
    blocks = prefill_cache.reshape(layers, slot_count, BLK, extent // BLK)
    blocks = jnp.where(live[None, :, :, None], blocks, jnp.zeros_like(blocks))
    blocks = blocks.reshape(layers, slot_count, extent).transpose(1, 0, 2)
    blocks = jnp.take(blocks, slot_of, axis=0)
    blocks = blocks.reshape(SIDE, SIDE, SIDE, layers, extent)
    return (blocks[..., :NEAR], blocks[..., NEAR:]), origin


def on_device(
    hidden_in, norm_gain, w_qkv, w_out, prefill_cache, lengths, prefill_table, decode_table
):
    layers, slot_count, kv_local, extent = prefill_cache.shape
    (cache_a, cache_b), origin = outgoing_blocks(
        prefill_cache, lengths, prefill_table, decode_table
    )
    weights, first_a = gather_tok(pack_weight(w_qkv, 4, 80), cache_a, 48)
    query, key_value = project(hidden_in, norm_gain, unpack_weight(weights, 4, *w_qkv.shape))
    context, out_all, *arrived = attend(
        query, key_value, pack_weight(w_out.T, 3, 64), first_a, cache_b
    )
    out_weight = unpack_weight(out_all, 3, w_out.shape[1], w_out.shape[0])
    part = jnp.dot(out_weight, context, preferred_element_type=jnp.float32).astype(jnp.bfloat16)
    heads = lax.axis_size("head")
    part = part.reshape(heads // 2, 2, part.shape[0] // heads, part.shape[1])
    attn_out = head_sum(part).T
    arrived = jnp.concatenate(arrived, axis=-1).reshape(slot_count, layers, extent)
    decode_cache = jnp.take(arrived, origin, axis=0).transpose(1, 0, 2)
    return attn_out, decode_cache.reshape(prefill_cache.shape)


def solution(mesh):
    in_specs = (
        P("tok", None),
        P(),
        P("tok", "head"),
        P("head", "tok"),
        P(None, "tok", "head", None),
        P(),
        P(),
        P(),
    )
    out_specs = (P("tok", "head"), P(None, "tok", "head", None))
    return jax.shard_map(
        on_device, mesh=mesh, in_specs=in_specs, out_specs=out_specs, check_vma=False
    )
```

```python
import functools
import math

import jax
import jax.numpy as jnp
from jax import lax
from jax.experimental import pallas as pl
from jax.experimental.pallas import tpu as pltpu
from jax.sharding import PartitionSpec as P

HD = 80
QPK = 4
BLK = 8
LANES = 128
NEAR = 4 * LANES
SIDE = 4

NORM_EPS = 1e-05
ROPE_BASE = 1000000.0
LOWEST = -1e30
EXP2_SCALE = math.log2(math.e) / math.sqrt(HD)

MESH = pl.DeviceIdType.MESH


def coordinates():
    index = lax.axis_index("tok")
    return index // 16, (index // 4) % 4, index % 4


def along(axis, step):
    place = list(coordinates())
    place[axis] = (place[axis] + step) % SIDE
    return (place[0] * SIDE + place[1]) * SIDE + place[2]


def greet(far):
    barrier = pltpu.get_barrier_semaphore()
    peers = [along(axis, step) for axis in range(3) for step in (1, 3)]
    peers += [along(axis, 2) for axis in far]
    for peer in peers:
        pl.semaphore_signal(barrier, inc=1, device_id={"tok": peer}, device_id_type=MESH)
    pl.semaphore_wait(barrier, len(peers))


def remote(src, dst, send_sem, recv_sem, peer):
    return pltpu.make_async_remote_copy(
        src_ref=src,
        dst_ref=dst,
        send_sem=send_sem,
        recv_sem=recv_sem,
        device_id={"tok": peer},
        device_id_type=MESH,
    )


ORDERS = ((0, 1, 2), (0, 2, 1))
FAR_ORDER = (1, 2, 0)


class Gather:
    def __init__(self, src, buf, split, send_sem, recv_sem, own_sem):
        self.src, self.buf, self.split = src, buf, split
        self.send_sem, self.recv_sem, self.own_sem = send_sem, recv_sem, own_sem
        self.sent = []

    def own(self):
        z, y, x = coordinates()
        for part in range(2):
            pltpu.make_async_copy(
                self.src.at[part], self.buf.at[part, z, y, x], self.own_sem.at[part]
            ).start()
        for part in range(2):
            pltpu.make_async_copy(
                self.src.at[part], self.buf.at[part, z, y, x], self.own_sem.at[part]
            ).wait()

    def view(self, part, phase, step, rows):
        done = ORDERS[part][:phase]
        axis = ORDERS[part][phase]
        place = list(coordinates())
        place[axis] = (place[axis] + step) % SIDE
        for seen in done:
            place[seen] = slice(None)
        return self.buf.at[(part, *place, rows, slice(None))]

    def copy(self, part, phase, which):
        axis = ORDERS[part][phase]
        every = slice(None)
        upper, lower = pl.ds(0, self.split), pl.ds(self.split, self.buf.shape[4] - self.split)
        step, rows, way = (
            (0, every, 1),
            (0, every, 3),
            (3, upper, 1),
            (1, lower, 3),
        )[which]
        view = self.view(part, phase, step, rows)
        return remote(
            view,
            view,
            self.send_sem.at[part, phase, which],
            self.recv_sem.at[part, phase, which],
            along(axis, way),
        )

    def start(self, phase):
        for part in range(2):
            for which in (0, 1):
                self.copy(part, phase, which).start()

    def pass_on(self, phase):
        for part in range(2):
            for which in (0, 1):
                self.copy(part, phase, which).wait_recv()
                self.copy(part, phase, which + 2).start()

    def finish(self, phase):
        for part in range(2):
            for which in (2, 3):
                self.copy(part, phase, which).wait_recv()

    def drain(self):
        for part in range(2):
            for phase in range(3):
                for which in range(4):
                    self.copy(part, phase, which).wait_send()


class Flow:
    def __init__(self, src, buf, split, z_send, z_recv, send_sem, recv_sem, own_sem):
        self.src, self.buf, self.split = src, buf, split
        self.z_send, self.z_recv = z_send, z_recv
        self.send_sem, self.recv_sem, self.own_sem = send_sem, recv_sem, own_sem

    def own(self):
        z, y, x = coordinates()
        copy = pltpu.make_async_copy(self.src, self.buf.at[:, z, y, x], self.own_sem)
        copy.start()
        copy.wait()

    def plan(self, which):
        upper, lower = pl.ds(0, self.split), pl.ds(self.split, self.buf.shape[4] - self.split)
        every = slice(None)
        return ((0, every, 1), (0, every, 3), (3, upper, 1), (1, lower, 3))[which]

    def z_copy(self, which):
        step, rows, way = self.plan(which)
        z, y, x = coordinates()
        view = self.buf.at[:, (z + step) % SIDE, y, x, rows, :]
        return remote(view, view, self.z_send.at[which], self.z_recv.at[which], along(0, way))

    def z_start(self):
        self.z_copy(0).start()
        self.z_copy(1).start()

    def z_pass_on(self):
        for which in (0, 1):
            self.z_copy(which).wait_recv()
            self.z_copy(which + 2).start()

    def z_finish(self):
        for which in (2, 3):
            self.z_copy(which).wait_recv()

    def copy(self, row, part, phase, which):
        step, rows, way = self.plan(which)
        axis = ORDERS[part][1 + phase]
        place = list(coordinates())
        place[0] = (place[0] + row) % SIDE
        place[axis] = (place[axis] + step) % SIDE
        if phase:
            place[ORDERS[part][1]] = slice(None)
        view = self.buf.at[(part, *place, rows, slice(None))]
        sem = (row, part, phase, which)
        return remote(view, view, self.send_sem.at[sem], self.recv_sem.at[sem], along(axis, way))

    def start(self, row, phase):
        for part in range(2):
            for which in (0, 1):
                self.copy(row, part, phase, which).start()

    def pass_on(self, row, phase):
        for part in range(2):
            for which in (0, 1):
                self.copy(row, part, phase, which).wait_recv()
                self.copy(row, part, phase, which + 2).start()

    def finish(self, row, phase):
        for part in range(2):
            for which in (2, 3):
                self.copy(row, part, phase, which).wait_recv()

    def drain(self):
        for which in range(4):
            self.z_copy(which).wait_send()
        for row in range(SIDE):
            for part in range(2):
                for phase in range(2):
                    for which in range(4):
                        self.copy(row, part, phase, which).wait_send()

    def head(self, beside):
        self.own()
        self.z_start()
        self.start(0, 0)
        self.pass_on(0, 0)
        self.finish(0, 0)
        self.start(0, 1)
        self.z_pass_on()
        beside()
        self.start(3, 0)
        self.start(1, 0)
        self.pass_on(0, 1)
        for row in (3, 1):
            self.pass_on(row, 0)
        for row in (3, 1):
            self.finish(row, 0)
            self.start(row, 1)
        self.finish(0, 1)


class Exchange:
    def __init__(self, order, phases, bufs, relay, send_sem, recv_sem, own_sem):
        self.order, self.phases, self.bufs, self.relay = order, phases, bufs, relay
        self.send_sem, self.recv_sem, self.own_sem = send_sem, recv_sem, own_sem

    def part(self, phase, buf, index, half):
        axis = self.order[phase]
        place = [slice(None)] * 3
        if half is not None:
            place[1 if axis == 0 else 0] = pl.ds(2 * half, 2)
        place[axis] = index
        return buf.at[tuple(place)]

    def own(self, phase):
        here = coordinates()[self.order[phase]]
        return pltpu.make_async_copy(
            self.part(phase, self.bufs[phase], here, None),
            self.part(phase, self.bufs[phase + 1], here, None),
            self.own_sem.at[phase],
        )

    def copy(self, phase, which):
        axis = self.order[phase]
        here = coordinates()[axis]
        src, dst = self.bufs[phase], self.bufs[phase + 1]
        sems = (self.send_sem.at[phase, which], self.recv_sem.at[phase, which])
        if which < 2:
            step = (1, 3)[which]
            there = (here + step) % SIDE
            return remote(
                self.part(phase, src, there, None),
                self.part(phase, dst, here, None),
                *sems,
                along(axis, step),
            )
        half = which % 2
        step = (1, 3)[half]
        relay = self.relay.at[phase - self.phases[0], half]
        if which < 4:
            there = (here + 2) % SIDE
            return remote(self.part(phase, src, there, half), relay, *sems, along(axis, step))
        origin = (here + 4 - step) % SIDE
        return remote(relay, self.part(phase, dst, origin, half), *sems, along(axis, step))

    def start(self, phase):
        self.own(phase).start()
        for which in (2, 3, 0, 1):
            self.copy(phase, which).start()

    def pass_on(self, phase):
        for which in (2, 3):
            self.copy(phase, which).wait_recv()
            self.copy(phase, which + 2).start()

    def finish(self, phase):
        self.own(phase).wait()
        for which in (0, 1, 4, 5):
            self.copy(phase, which).wait_recv()

    def drain(self):
        for phase in self.phases:
            for which in range(6):
                self.copy(phase, which).wait_send()


def relay_buffer(block, phases):
    return pltpu.VMEM((phases, 2, 2, SIDE, *block.shape[3:]), block.dtype)


def gather_kernel(
    split, src, near_src, far_src, buf, near_dst, far_dst, far_first, near_relay, far_relay, *sems
):
    greet(())
    gather = Flow(src, buf, split, *sems[0:5])
    near = Exchange(ORDERS[0], (0,), (near_src, near_dst), near_relay, *sems[5:8])
    far = Exchange(FAR_ORDER, (0, 1), (far_src, far_first, far_dst), far_relay, *sems[8:11])

    def beside():
        near.start(0)
        far.start(0)

    gather.head(beside)
    gather.z_finish()
    gather.start(2, 0)
    for row in (3, 1):
        gather.pass_on(row, 1)
    far.pass_on(0)
    gather.pass_on(2, 0)
    gather.finish(2, 0)
    gather.start(2, 1)
    for row in (3, 1):
        gather.finish(row, 1)
    far.finish(0)
    far.start(1)
    gather.pass_on(2, 1)
    near.pass_on(0)
    far.pass_on(1)
    gather.finish(2, 1)
    near.finish(0)
    far.finish(1)
    gather.drain()
    near.drain()
    far.drain()


def flow_sems():
    return [
        pltpu.SemaphoreType.DMA((4,)),
        pltpu.SemaphoreType.DMA((4,)),
        pltpu.SemaphoreType.DMA((SIDE, 2, 2, 4)),
        pltpu.SemaphoreType.DMA((SIDE, 2, 2, 4)),
        pltpu.SemaphoreType.DMA,
    ]


def gather_sems():
    return [
        pltpu.SemaphoreType.DMA((2, 3, 4)),
        pltpu.SemaphoreType.DMA((2, 3, 4)),
        pltpu.SemaphoreType.DMA((2,)),
    ]


def exchange_sems():
    return [
        pltpu.SemaphoreType.DMA((3, 6)),
        pltpu.SemaphoreType.DMA((3, 6)),
        pltpu.SemaphoreType.DMA((3,)),
    ]


VMEM_SPEC = pl.BlockSpec(memory_space=pltpu.VMEM)


def like(block):
    return jax.ShapeDtypeStruct(block.shape, block.dtype)


def gathered(block):
    return jax.ShapeDtypeStruct((2, SIDE, SIDE, SIDE, block.shape[1], LANES), block.dtype)


def gather_tok(block, near, far, split):
    return pl.pallas_call(
        functools.partial(gather_kernel, split),
        out_shape=(gathered(block), like(near), like(far)),
        in_specs=[VMEM_SPEC] * 3,
        out_specs=[VMEM_SPEC] * 3,
        scratch_shapes=[
            pltpu.VMEM(far.shape, far.dtype),
            relay_buffer(near, 1),
            relay_buffer(far, 2),
            *flow_sems(),
            *exchange_sems(),
            *exchange_sems(),
        ],
        compiler_params=pltpu.CompilerParams(collective_id=0, has_side_effects=True),
        name="gather_tok",
    )(block, near, far)


def attend_group(z, y, masked, query, kv, top, total, weighted):
    places = [(part, x) for x in range(SIDE) for part in range(2)]
    key = jnp.concatenate([kv[part, z, y, x, :HD, :] for part, x in places], axis=1)
    value = jnp.concatenate([kv[part, z, y, x, HD:, :] for part, x in places], axis=1)
    width = query.shape[1] // QPK
    if masked:
        shape = (LANES, width)
        ahead = lax.broadcasted_iota(jnp.int32, shape, 0) - lax.broadcasted_iota(
            jnp.int32, shape, 1
        )
        my_x = coordinates()[2]
        behind = [(my_x - x) * width - part * LANES for part, x in places]
    for head in range(QPK):
        cols = pl.ds(head * width, width)
        score = lax.dot_general(
            key, query[:, cols], (((0,), (0,)), ((), ())), preferred_element_type=jnp.float32
        )
        if masked:
            score = jnp.concatenate(
                [
                    jnp.where(
                        ahead <= limit, score[place * LANES : (place + 1) * LANES], LOWEST
                    )
                    for place, limit in enumerate(behind)
                ],
                axis=0,
            )
        before = top[:, cols]
        highest = jnp.maximum(before, jnp.max(score, axis=0, keepdims=True))
        expo = jnp.exp2((score - highest) * EXP2_SCALE)
        shrink = jnp.exp2((before - highest) * EXP2_SCALE)
        total[:, cols] = total[:, cols] * shrink + jnp.sum(expo, axis=0, keepdims=True)
        weighted[:, cols] = weighted[:, cols] * shrink + jnp.dot(
            value, expo.astype(jnp.bfloat16), preferred_element_type=jnp.float32
        )
        top[:, cols] = highest


def attend_kernel(
    query,
    kv_src,
    out_src,
    near_first,
    far_second,
    context,
    out_buf,
    near_dst,
    far_dst,
    kv_buf,
    near_second,
    near_relay,
    far_relay,
    top,
    total,
    weighted,
    *sems,
):
    greet(())
    kv = Flow(kv_src, kv_buf, HD, *sems[0:5])
    out = Gather(out_src, out_buf, 32, *sems[5:8])
    near = Exchange(
        ORDERS[0], (1, 2), (None, near_first, near_second, near_dst), near_relay, *sems[8:11]
    )
    far = Exchange(FAR_ORDER, (2,), (None, None, far_second, far_dst), far_relay, *sems[11:14])
    my_z, my_y, _ = coordinates()
    state = (query, kv_buf, top, total, weighted)

    def groups(z, low, count):
        def step(y, carry):
            attend_group(z, y, False, *state)
            return carry

        lax.fori_loop(low, low + count, step, 0)

    def row(step, half):
        earlier = my_z // (SIDE - step)
        earlier = jnp.minimum(earlier, 1)
        groups((my_z + step) % SIDE, 2 * half, 2 * earlier)

    top[...] = jnp.full_like(top, LOWEST)
    total[...] = jnp.zeros_like(total)
    weighted[...] = jnp.zeros_like(weighted)
    kv.head(lambda: far.start(2))
    out.own()
    attend_group(my_z, my_y, True, *state)
    kv.z_finish()
    kv.start(2, 0)
    out.start(0)
    groups(my_z, 0, my_y)
    for way in (3, 1):
        kv.pass_on(way, 1)
    kv.pass_on(2, 0)
    kv.finish(2, 0)
    kv.start(2, 1)
    near.start(1)
    out.pass_on(0)
    kv.finish(3, 1)
    row(3, 0)
    kv.pass_on(2, 1)
    far.pass_on(2)
    near.pass_on(1)
    out.finish(0)
    out.start(1)
    row(3, 1)
    kv.finish(1, 1)
    kv.finish(2, 1)
    out.pass_on(1)
    near.finish(1)
    near.start(2)
    row(1, 0)
    near.pass_on(2)
    out.finish(1)
    out.start(2)
    row(1, 1)
    out.pass_on(2)
    row(2, 0)
    row(2, 1)
    width = query.shape[1] // QPK
    for head in range(QPK):
        cols = pl.ds(head * width, width)
        context[pl.ds(head * HD, HD), :] = (weighted[:, cols] / total[:, cols]).astype(
            context.dtype
        )
    near.finish(2)
    far.finish(2)
    out.finish(2)
    kv.drain()
    out.drain()
    near.drain()
    far.drain()


def attend(query, kv_block, out_block, near, far):
    columns = query.shape[1]
    return pl.pallas_call(
        attend_kernel,
        out_shape=(
            jax.ShapeDtypeStruct((QPK * HD, columns // QPK), jnp.bfloat16),
            gathered(out_block),
            like(near),
            like(far),
        ),
        in_specs=[VMEM_SPEC] * 5,
        out_specs=[VMEM_SPEC] * 4,
        scratch_shapes=[
            pltpu.VMEM(gathered(kv_block).shape, kv_block.dtype),
            pltpu.VMEM(near.shape, near.dtype),
            relay_buffer(near, 2),
            relay_buffer(far, 1),
            pltpu.VMEM((1, columns), jnp.float32),
            pltpu.VMEM((1, columns), jnp.float32),
            pltpu.VMEM((HD, columns), jnp.float32),
            *flow_sems(),
            *gather_sems(),
            *exchange_sems(),
            *exchange_sems(),
        ],
        compiler_params=pltpu.CompilerParams(collective_id=1, has_side_effects=True),
        name="attend",
    )(query, kv_block, out_block, near, far)


def head_sum_kernel(part, result, swapped, pair, arrived, swap_sem, send_sem, recv_sem):
    index = lax.axis_index("head")
    chip, core = index // 2, index % 2
    partner = chip * 2 + 1 - core
    others = [((chip + step) % SIDE) * 2 + core for step in (1, 2, 3)]
    barrier = pltpu.get_barrier_semaphore()
    for peer in (partner, *others):
        pl.semaphore_signal(barrier, inc=1, device_id={"head": peer}, device_id_type=MESH)
    pl.semaphore_wait(barrier, 4)

    def to_partner(step):
        return pltpu.make_async_remote_copy(
            src_ref=part.at[(chip + step) % SIDE, 1 - core],
            dst_ref=swapped.at[step],
            send_sem=swap_sem.at[0, step],
            recv_sem=swap_sem.at[1, step],
            device_id={"head": partner},
            device_id_type=MESH,
        )

    def to_chip(step):
        return pltpu.make_async_remote_copy(
            src_ref=pair.at[step],
            dst_ref=arrived.at[step],
            send_sem=send_sem.at[step],
            recv_sem=recv_sem.at[step],
            device_id={"head": others[step - 1]},
            device_id_type=MESH,
        )

    def add(step):
        mine = part[(chip + step) % SIDE, core].astype(jnp.float32)
        return mine + swapped[step].astype(jnp.float32)

    order = (2, 1, 3)
    for step in (*order, 0):
        to_partner(step).start()
    for place, step in enumerate(order):
        to_partner(step).wait_recv()
        pair[step] = add(step).astype(pair.dtype)
        if place:
            to_chip(order[place - 1]).start()
    to_partner(0).wait_recv()
    pair[0] = add(0).astype(pair.dtype)
    to_chip(order[-1]).start()
    whole = pair[0].astype(jnp.float32)
    for step in (1, 3, 2):
        to_chip(step).wait_recv()
        whole = whole + arrived[step].astype(jnp.float32)
    result[...] = whole.astype(result.dtype)
    for step in order:
        to_chip(step).wait_send()
    for step in range(SIDE):
        to_partner(step).wait_send()


def head_sum(part):
    slices = pltpu.VMEM((SIDE, *part.shape[2:]), part.dtype)
    return pl.pallas_call(
        head_sum_kernel,
        out_shape=jax.ShapeDtypeStruct(part.shape[2:], part.dtype),
        in_specs=[VMEM_SPEC],
        out_specs=VMEM_SPEC,
        scratch_shapes=[
            slices,
            slices,
            slices,
            pltpu.SemaphoreType.DMA((2, SIDE)),
            pltpu.SemaphoreType.DMA((SIDE,)),
            pltpu.SemaphoreType.DMA((SIDE,)),
        ],
        compiler_params=pltpu.CompilerParams(collective_id=2, has_side_effects=True),
        name="head_sum",
    )(part)


def pack_weight(block, lane_chunks, rows):
    height, width = block.shape
    block = jnp.pad(block, ((0, 0), (0, lane_chunks * LANES - width)))
    block = block.reshape(height, lane_chunks, LANES).transpose(1, 0, 2)
    block = block.reshape(lane_chunks * height, LANES)
    block = jnp.pad(block, ((0, 2 * rows - lane_chunks * height), (0, 0)))
    return block.reshape(2, rows, LANES)


def unpack_weight(buf, lane_chunks, height, width):
    rows = buf.shape[4]
    count = SIDE * SIDE * SIDE
    buf = buf.reshape(2, count, rows, LANES).transpose(1, 0, 2, 3)
    buf = buf.reshape(count, 2 * rows, LANES)[:, : lane_chunks * height]
    buf = buf.reshape(count, lane_chunks, height, LANES).transpose(0, 2, 1, 3)
    return buf.reshape(count * height, lane_chunks * LANES)[:, :width]


def project(hidden_in, norm_gain, weight):
    tok_rows = hidden_in.shape[0]
    float_rows = hidden_in.astype(jnp.float32)
    normed = (
        float_rows
        * lax.rsqrt(jnp.mean(float_rows * float_rows, axis=-1, keepdims=True) + NORM_EPS)
        * norm_gain
    ).astype(jnp.bfloat16)
    projected = lax.dot_general(
        weight, normed, (((0,), (1,)), ((), ())), preferred_element_type=jnp.float32
    ).reshape(QPK + 2, HD, tok_rows)
    half = HD // 2
    frequency = ROPE_BASE ** (-2.0 * jnp.arange(half, dtype=jnp.float32) / HD)
    positions = lax.axis_index("tok") * tok_rows + jnp.arange(tok_rows, dtype=jnp.int32)
    angles = frequency[:, None] * positions.astype(jnp.float32)[None, :]
    cosine, sines = jnp.cos(angles)[None], jnp.sin(angles)[None]
    front, back = projected[: QPK + 1, :half], projected[: QPK + 1, half:]
    turned = jnp.concatenate(
        [front * cosine - back * sines, back * cosine + front * sines], axis=1
    ).astype(jnp.bfloat16)
    query = turned[:QPK].transpose(1, 0, 2).reshape(HD, QPK * tok_rows)
    key_value = jnp.concatenate([turned[QPK], projected[QPK + 1].astype(jnp.bfloat16)], axis=0)
    key_value = key_value.reshape(2 * HD, 2, LANES).transpose(1, 0, 2)
    return query, key_value


def outgoing_blocks(prefill_cache, lengths, prefill_table, decode_table):
    tok_count = lax.axis_size("tok")
    my_index = lax.axis_index("tok")
    layers, slot_count, _, extent = prefill_cache.shape
    block_total = prefill_table.shape[0]
    per_request = block_total // lengths.shape[0]
    every_block = jnp.arange(block_total, dtype=jnp.int32)
    slots = jnp.arange(slot_count, dtype=jnp.int32)
    mine = prefill_table[:, None] == (my_index * slot_count + slots)[None, :]
    held_here = jnp.sum(jnp.where(mine, every_block[:, None], 0), axis=0)
    target = jnp.sum(jnp.where(mine, (decode_table // slot_count)[:, None], 0), axis=0)
    request = held_here // per_request
    requests = jnp.arange(lengths.shape[0], dtype=jnp.int32)
    request_len = jnp.sum(
        jnp.where(request[:, None] == requests[None, :], lengths[None, :], 0), axis=1
    )
    first_token = held_here % per_request * BLK
    live = first_token[:, None] + jnp.arange(BLK, dtype=jnp.int32)[None, :] < request_len[:, None]
    peers = jnp.arange(tok_count, dtype=jnp.int32)
    slot_of = jnp.sum(jnp.where(target[None, :] == peers[:, None], slots[None, :], 0), axis=1)
    origin = (my_index - (target - my_index)) % tok_count
    blocks = prefill_cache.reshape(layers, slot_count, BLK, extent // BLK)
    blocks = jnp.where(live[None, :, :, None], blocks, jnp.zeros_like(blocks))
    blocks = blocks.reshape(layers, slot_count, extent).transpose(1, 0, 2)
    blocks = jnp.take(blocks, slot_of, axis=0)
    blocks = blocks.reshape(SIDE, SIDE, SIDE, layers, extent)
    return (blocks[..., :NEAR], blocks[..., NEAR:]), origin


def on_device(
    hidden_in, norm_gain, w_qkv, w_out, prefill_cache, lengths, prefill_table, decode_table
):
    layers, slot_count, kv_local, extent = prefill_cache.shape
    (near, far), origin = outgoing_blocks(
        prefill_cache, lengths, prefill_table, decode_table
    )
    weights, near, far = gather_tok(pack_weight(w_qkv, 4, 80), near, far, 48)
    query, key_value = project(hidden_in, norm_gain, unpack_weight(weights, 4, *w_qkv.shape))
    context, out_all, *arrived = attend(
        query, key_value, pack_weight(w_out.T, 3, 64), near, far
    )
    out_weight = unpack_weight(out_all, 3, w_out.shape[1], w_out.shape[0])
    part = jnp.dot(out_weight, context, preferred_element_type=jnp.float32).astype(jnp.bfloat16)
    heads = lax.axis_size("head")
    part = part.reshape(heads // 2, 2, part.shape[0] // heads, part.shape[1])
    attn_out = head_sum(part).T
    arrived = jnp.concatenate(arrived, axis=-1).reshape(slot_count, layers, extent)
    decode_cache = jnp.take(arrived, origin, axis=0).transpose(1, 0, 2)
    return attn_out, decode_cache.reshape(prefill_cache.shape)


def solution(mesh):
    in_specs = (
        P("tok", None),
        P(),
        P("tok", "head"),
        P("head", "tok"),
        P(None, "tok", "head", None),
        P(),
        P(),
        P(),
    )
    out_specs = (P("tok", "head"), P(None, "tok", "head", None))
    return jax.shard_map(
        on_device, mesh=mesh, in_specs=in_specs, out_specs=out_specs, check_vma=False
    )
```

```python
import functools
import math

import jax
import jax.numpy as jnp
from jax import lax
from jax.experimental import pallas as pl
from jax.experimental.pallas import tpu as pltpu
from jax.sharding import PartitionSpec as P

HD = 80
QPK = 4
BLK = 8
LANES = 128
NEAR = 4 * LANES
SIDE = 4

NORM_EPS = 1e-05
ROPE_BASE = 1000000.0
LOWEST = -1e30
EXP2_SCALE = math.log2(math.e) / math.sqrt(HD)

MESH = pl.DeviceIdType.MESH


def coordinates():
    index = lax.axis_index("tok")
    return index // 16, (index // 4) % 4, index % 4


def along(axis, step):
    place = list(coordinates())
    place[axis] = (place[axis] + step) % SIDE
    return (place[0] * SIDE + place[1]) * SIDE + place[2]


def greet(far):
    barrier = pltpu.get_barrier_semaphore()
    peers = [along(axis, step) for axis in range(3) for step in (1, 3)]
    peers += [along(axis, 2) for axis in far]
    for peer in peers:
        pl.semaphore_signal(barrier, inc=1, device_id={"tok": peer}, device_id_type=MESH)
    pl.semaphore_wait(barrier, len(peers))


def remote(src, dst, send_sem, recv_sem, peer):
    return pltpu.make_async_remote_copy(
        src_ref=src,
        dst_ref=dst,
        send_sem=send_sem,
        recv_sem=recv_sem,
        device_id={"tok": peer},
        device_id_type=MESH,
    )


ORDERS = ((0, 1, 2), (0, 2, 1))
FAR_ORDER = (1, 2, 0)


class Gather:
    def __init__(self, src, buf, split, send_sem, recv_sem, own_sem):
        self.src, self.buf, self.split = src, buf, split
        self.send_sem, self.recv_sem, self.own_sem = send_sem, recv_sem, own_sem
        self.sent = []

    def own(self):
        z, y, x = coordinates()
        for part in range(2):
            pltpu.make_async_copy(
                self.src.at[part], self.buf.at[part, z, y, x], self.own_sem.at[part]
            ).start()
        for part in range(2):
            pltpu.make_async_copy(
                self.src.at[part], self.buf.at[part, z, y, x], self.own_sem.at[part]
            ).wait()

    def view(self, part, phase, step, rows):
        done = ORDERS[part][:phase]
        axis = ORDERS[part][phase]
        place = list(coordinates())
        place[axis] = (place[axis] + step) % SIDE
        for seen in done:
            place[seen] = slice(None)
        return self.buf.at[(part, *place, rows, slice(None))]

    def copy(self, part, phase, which):
        axis = ORDERS[part][phase]
        every = slice(None)
        upper, lower = pl.ds(0, self.split), pl.ds(self.split, self.buf.shape[4] - self.split)
        step, rows, way = (
            (0, every, 1),
            (0, every, 3),
            (3, upper, 1),
            (1, lower, 3),
        )[which]
        view = self.view(part, phase, step, rows)
        return remote(
            view,
            view,
            self.send_sem.at[part, phase, which],
            self.recv_sem.at[part, phase, which],
            along(axis, way),
        )

    def start(self, phase):
        for part in range(2):
            for which in (0, 1):
                self.copy(part, phase, which).start()

    def pass_on(self, phase):
        for part in range(2):
            for which in (0, 1):
                self.copy(part, phase, which).wait_recv()
                self.copy(part, phase, which + 2).start()

    def finish(self, phase):
        for part in range(2):
            for which in (2, 3):
                self.copy(part, phase, which).wait_recv()

    def drain(self):
        for part in range(2):
            for phase in range(3):
                for which in range(4):
                    self.copy(part, phase, which).wait_send()


class Flow:
    def __init__(self, src, buf, split, z_send, z_recv, send_sem, recv_sem, own_sem):
        self.src, self.buf, self.split = src, buf, split
        self.z_send, self.z_recv = z_send, z_recv
        self.send_sem, self.recv_sem, self.own_sem = send_sem, recv_sem, own_sem

    def own(self):
        z, y, x = coordinates()
        copy = pltpu.make_async_copy(self.src, self.buf.at[:, z, y, x], self.own_sem)
        copy.start()
        copy.wait()

    def plan(self, which):
        upper, lower = pl.ds(0, self.split), pl.ds(self.split, self.buf.shape[4] - self.split)
        every = slice(None)
        return ((0, every, 1), (0, every, 3), (3, upper, 1), (1, lower, 3))[which]

    def z_copy(self, which):
        step, rows, way = self.plan(which)
        z, y, x = coordinates()
        view = self.buf.at[:, (z + step) % SIDE, y, x, rows, :]
        return remote(view, view, self.z_send.at[which], self.z_recv.at[which], along(0, way))

    def z_start(self):
        self.z_copy(0).start()
        self.z_copy(1).start()

    def z_pass_on(self):
        for which in (0, 1):
            self.z_copy(which).wait_recv()
            self.z_copy(which + 2).start()

    def z_finish(self):
        for which in (2, 3):
            self.z_copy(which).wait_recv()

    def copy(self, row, part, phase, which):
        step, rows, way = self.plan(which)
        axis = ORDERS[part][1 + phase]
        place = list(coordinates())
        place[0] = (place[0] + row) % SIDE
        place[axis] = (place[axis] + step) % SIDE
        if phase:
            place[ORDERS[part][1]] = slice(None)
        view = self.buf.at[(part, *place, rows, slice(None))]
        sem = (row, part, phase, which)
        return remote(view, view, self.send_sem.at[sem], self.recv_sem.at[sem], along(axis, way))

    def start(self, row, phase):
        for part in range(2):
            for which in (0, 1):
                self.copy(row, part, phase, which).start()

    def pass_on(self, row, phase):
        for part in range(2):
            for which in (0, 1):
                self.copy(row, part, phase, which).wait_recv()
                self.copy(row, part, phase, which + 2).start()

    def finish(self, row, phase):
        for part in range(2):
            for which in (2, 3):
                self.copy(row, part, phase, which).wait_recv()

    def drain(self):
        for which in range(4):
            self.z_copy(which).wait_send()
        for row in range(SIDE):
            for part in range(2):
                for phase in range(2):
                    for which in range(4):
                        self.copy(row, part, phase, which).wait_send()

    def head(self, beside):
        self.start(0, 0)
        self.pass_on(0, 0)
        self.finish(0, 0)
        self.start(0, 1)
        self.z_pass_on()
        beside()
        self.start(3, 0)
        self.start(1, 0)
        self.pass_on(0, 1)
        for row in (3, 1):
            self.pass_on(row, 0)
        for row in (3, 1):
            self.finish(row, 0)
            self.start(row, 1)
        self.finish(0, 1)


class Exchange:
    def __init__(self, order, phases, bufs, relay, send_sem, recv_sem, own_sem):
        self.order, self.phases, self.bufs, self.relay = order, phases, bufs, relay
        self.send_sem, self.recv_sem, self.own_sem = send_sem, recv_sem, own_sem

    def part(self, phase, buf, index, half):
        axis = self.order[phase]
        place = [slice(None)] * 3
        if half is not None:
            place[1 if axis == 0 else 0] = pl.ds(2 * half, 2)
        place[axis] = index
        return buf.at[tuple(place)]

    def own(self, phase):
        here = coordinates()[self.order[phase]]
        return pltpu.make_async_copy(
            self.part(phase, self.bufs[phase], here, None),
            self.part(phase, self.bufs[phase + 1], here, None),
            self.own_sem.at[phase],
        )

    def copy(self, phase, which):
        axis = self.order[phase]
        here = coordinates()[axis]
        src, dst = self.bufs[phase], self.bufs[phase + 1]
        sems = (self.send_sem.at[phase, which], self.recv_sem.at[phase, which])
        if which < 2:
            step = (1, 3)[which]
            there = (here + step) % SIDE
            return remote(
                self.part(phase, src, there, None),
                self.part(phase, dst, here, None),
                *sems,
                along(axis, step),
            )
        half = which % 2
        step = (1, 3)[half]
        relay = self.relay.at[phase - self.phases[0], half]
        if which < 4:
            there = (here + 2) % SIDE
            return remote(self.part(phase, src, there, half), relay, *sems, along(axis, step))
        origin = (here + 4 - step) % SIDE
        return remote(relay, self.part(phase, dst, origin, half), *sems, along(axis, step))

    def start(self, phase):
        self.own(phase).start()
        for which in (2, 3, 0, 1):
            self.copy(phase, which).start()

    def pass_on(self, phase):
        for which in (2, 3):
            self.copy(phase, which).wait_recv()
            self.copy(phase, which + 2).start()

    def finish(self, phase):
        self.own(phase).wait()
        for which in (0, 1, 4, 5):
            self.copy(phase, which).wait_recv()

    def drain(self):
        for phase in self.phases:
            for which in range(6):
                self.copy(phase, which).wait_send()


def relay_buffer(block, phases):
    return pltpu.VMEM((phases, 2, 2, SIDE, *block.shape[3:]), block.dtype)


def gather_kernel(
    split, src, near_src, far_src, buf, near_dst, far_dst, far_first, near_relay, far_relay, *sems
):
    greet(())
    gather = Flow(src, buf, split, *sems[0:5])
    near = Exchange(ORDERS[0], (0,), (near_src, near_dst), near_relay, *sems[5:8])
    far = Exchange(FAR_ORDER, (0, 1), (far_src, far_first, far_dst), far_relay, *sems[8:11])

    def beside():
        near.start(0)
        far.start(0)

    gather.own()
    gather.z_start()
    gather.head(beside)
    gather.z_finish()
    gather.start(2, 0)
    for row in (3, 1):
        gather.pass_on(row, 1)
    far.pass_on(0)
    gather.pass_on(2, 0)
    gather.finish(2, 0)
    gather.start(2, 1)
    for row in (3, 1):
        gather.finish(row, 1)
    far.finish(0)
    far.start(1)
    gather.pass_on(2, 1)
    near.pass_on(0)
    far.pass_on(1)
    gather.finish(2, 1)
    near.finish(0)
    far.finish(1)
    gather.drain()
    near.drain()
    far.drain()


def flow_sems():
    return [
        pltpu.SemaphoreType.DMA((4,)),
        pltpu.SemaphoreType.DMA((4,)),
        pltpu.SemaphoreType.DMA((SIDE, 2, 2, 4)),
        pltpu.SemaphoreType.DMA((SIDE, 2, 2, 4)),
        pltpu.SemaphoreType.DMA,
    ]


def gather_sems():
    return [
        pltpu.SemaphoreType.DMA((2, 3, 4)),
        pltpu.SemaphoreType.DMA((2, 3, 4)),
        pltpu.SemaphoreType.DMA((2,)),
    ]


def exchange_sems():
    return [
        pltpu.SemaphoreType.DMA((3, 6)),
        pltpu.SemaphoreType.DMA((3, 6)),
        pltpu.SemaphoreType.DMA((3,)),
    ]


VMEM_SPEC = pl.BlockSpec(memory_space=pltpu.VMEM)


def like(block):
    return jax.ShapeDtypeStruct(block.shape, block.dtype)


def gathered(block):
    return jax.ShapeDtypeStruct((2, SIDE, SIDE, SIDE, block.shape[1], LANES), block.dtype)


def gather_tok(block, near, far, split):
    return pl.pallas_call(
        functools.partial(gather_kernel, split),
        out_shape=(gathered(block), like(near), like(far)),
        in_specs=[VMEM_SPEC] * 3,
        out_specs=[VMEM_SPEC] * 3,
        scratch_shapes=[
            pltpu.VMEM(far.shape, far.dtype),
            relay_buffer(near, 1),
            relay_buffer(far, 2),
            *flow_sems(),
            *exchange_sems(),
            *exchange_sems(),
        ],
        compiler_params=pltpu.CompilerParams(collective_id=0, has_side_effects=True),
        name="gather_tok",
    )(block, near, far)


def attend_group(z, y, masked, query, kv, top, total, weighted):
    places = [(part, x) for x in range(SIDE) for part in range(2)]
    key = jnp.concatenate([kv[part, z, y, x, :HD, :] for part, x in places], axis=1)
    value = jnp.concatenate([kv[part, z, y, x, HD:, :] for part, x in places], axis=1)
    width = query.shape[1] // QPK
    if masked:
        shape = (LANES, width)
        ahead = lax.broadcasted_iota(jnp.int32, shape, 0) - lax.broadcasted_iota(
            jnp.int32, shape, 1
        )
        my_x = coordinates()[2]
        behind = [(my_x - x) * width - part * LANES for part, x in places]
    for head in range(QPK):
        cols = pl.ds(head * width, width)
        score = lax.dot_general(
            key, query[:, cols], (((0,), (0,)), ((), ())), preferred_element_type=jnp.float32
        )
        if masked:
            score = jnp.concatenate(
                [
                    jnp.where(
                        ahead <= limit, score[place * LANES : (place + 1) * LANES], LOWEST
                    )
                    for place, limit in enumerate(behind)
                ],
                axis=0,
            )
        before = top[:, cols]
        highest = jnp.maximum(before, jnp.max(score, axis=0, keepdims=True))
        expo = jnp.exp2((score - highest) * EXP2_SCALE)
        shrink = jnp.exp2((before - highest) * EXP2_SCALE)
        total[:, cols] = total[:, cols] * shrink + jnp.sum(expo, axis=0, keepdims=True)
        weighted[:, cols] = weighted[:, cols] * shrink + jnp.dot(
            value, expo.astype(jnp.bfloat16), preferred_element_type=jnp.float32
        )
        top[:, cols] = highest


def attend_kernel(
    query,
    kv_src,
    out_src,
    near_first,
    far_second,
    context,
    out_buf,
    near_dst,
    far_dst,
    kv_buf,
    near_second,
    near_relay,
    far_relay,
    top,
    total,
    weighted,
    *sems,
):
    greet(())
    kv = Flow(kv_src, kv_buf, HD, *sems[0:5])
    out = Gather(out_src, out_buf, 32, *sems[5:8])
    near = Exchange(
        ORDERS[0], (1, 2), (None, near_first, near_second, near_dst), near_relay, *sems[8:11]
    )
    far = Exchange(FAR_ORDER, (2,), (None, None, far_second, far_dst), far_relay, *sems[11:14])
    my_z, my_y, _ = coordinates()
    state = (query, kv_buf, top, total, weighted)

    def groups(z, low, count):
        def step(y, carry):
            attend_group(z, y, False, *state)
            return carry

        lax.fori_loop(low, low + count, step, 0)

    def row(step, half):
        earlier = my_z // (SIDE - step)
        earlier = jnp.minimum(earlier, 1)
        groups((my_z + step) % SIDE, 2 * half, 2 * earlier)

    top[...] = jnp.full_like(top, LOWEST)
    total[...] = jnp.zeros_like(total)
    weighted[...] = jnp.zeros_like(weighted)
    def beside():
        out.pass_on(0)
        far.start(2)

    out.own()
    kv.own()
    kv.z_start()
    out.start(0)
    kv.head(beside)
    attend_group(my_z, my_y, True, *state)
    kv.z_finish()
    kv.start(2, 0)
    groups(my_z, 0, my_y)
    for way in (3, 1):
        kv.pass_on(way, 1)
    kv.pass_on(2, 0)
    kv.finish(2, 0)
    kv.start(2, 1)
    out.finish(0)
    out.start(1)
    near.start(1)
    kv.finish(3, 1)
    row(3, 0)
    kv.pass_on(2, 1)
    row(3, 1)
    kv.finish(1, 1)
    out.pass_on(1)
    near.pass_on(1)
    row(1, 0)
    far.pass_on(2)
    near.finish(1)
    near.start(2)
    out.finish(1)
    out.start(2)
    row(1, 1)
    near.pass_on(2)
    out.pass_on(2)
    kv.finish(2, 1)
    row(2, 0)
    row(2, 1)
    width = query.shape[1] // QPK
    for head in range(QPK):
        cols = pl.ds(head * width, width)
        context[pl.ds(head * HD, HD), :] = (weighted[:, cols] / total[:, cols]).astype(
            context.dtype
        )
    near.finish(2)
    far.finish(2)
    out.finish(2)
    kv.drain()
    out.drain()
    near.drain()
    far.drain()


def attend(query, kv_block, out_block, near, far):
    columns = query.shape[1]
    return pl.pallas_call(
        attend_kernel,
        out_shape=(
            jax.ShapeDtypeStruct((QPK * HD, columns // QPK), jnp.bfloat16),
            gathered(out_block),
            like(near),
            like(far),
        ),
        in_specs=[VMEM_SPEC] * 5,
        out_specs=[VMEM_SPEC] * 4,
        scratch_shapes=[
            pltpu.VMEM(gathered(kv_block).shape, kv_block.dtype),
            pltpu.VMEM(near.shape, near.dtype),
            relay_buffer(near, 2),
            relay_buffer(far, 1),
            pltpu.VMEM((1, columns), jnp.float32),
            pltpu.VMEM((1, columns), jnp.float32),
            pltpu.VMEM((HD, columns), jnp.float32),
            *flow_sems(),
            *gather_sems(),
            *exchange_sems(),
            *exchange_sems(),
        ],
        compiler_params=pltpu.CompilerParams(collective_id=1, has_side_effects=True),
        name="attend",
    )(query, kv_block, out_block, near, far)


def head_sum_kernel(part, result, swapped, pair, arrived, swap_sem, send_sem, recv_sem):
    index = lax.axis_index("head")
    chip, core = index // 2, index % 2
    partner = chip * 2 + 1 - core
    others = [((chip + step) % SIDE) * 2 + core for step in (1, 2, 3)]
    barrier = pltpu.get_barrier_semaphore()
    for peer in (partner, *others):
        pl.semaphore_signal(barrier, inc=1, device_id={"head": peer}, device_id_type=MESH)
    pl.semaphore_wait(barrier, 4)

    def to_partner(step):
        return pltpu.make_async_remote_copy(
            src_ref=part.at[(chip + step) % SIDE, 1 - core],
            dst_ref=swapped.at[step],
            send_sem=swap_sem.at[0, step],
            recv_sem=swap_sem.at[1, step],
            device_id={"head": partner},
            device_id_type=MESH,
        )

    def to_chip(step):
        return pltpu.make_async_remote_copy(
            src_ref=pair.at[step],
            dst_ref=arrived.at[step],
            send_sem=send_sem.at[step],
            recv_sem=recv_sem.at[step],
            device_id={"head": others[step - 1]},
            device_id_type=MESH,
        )

    def add(step):
        mine = part[(chip + step) % SIDE, core].astype(jnp.float32)
        return mine + swapped[step].astype(jnp.float32)

    order = (2, 1, 3)
    for step in (*order, 0):
        to_partner(step).start()
    for place, step in enumerate(order):
        to_partner(step).wait_recv()
        pair[step] = add(step).astype(pair.dtype)
        if place:
            to_chip(order[place - 1]).start()
    to_partner(0).wait_recv()
    pair[0] = add(0).astype(pair.dtype)
    to_chip(order[-1]).start()
    whole = pair[0].astype(jnp.float32)
    for step in (1, 3, 2):
        to_chip(step).wait_recv()
        whole = whole + arrived[step].astype(jnp.float32)
    result[...] = whole.astype(result.dtype)
    for step in order:
        to_chip(step).wait_send()
    for step in range(SIDE):
        to_partner(step).wait_send()


def head_sum(part):
    slices = pltpu.VMEM((SIDE, *part.shape[2:]), part.dtype)
    return pl.pallas_call(
        head_sum_kernel,
        out_shape=jax.ShapeDtypeStruct(part.shape[2:], part.dtype),
        in_specs=[VMEM_SPEC],
        out_specs=VMEM_SPEC,
        scratch_shapes=[
            slices,
            slices,
            slices,
            pltpu.SemaphoreType.DMA((2, SIDE)),
            pltpu.SemaphoreType.DMA((SIDE,)),
            pltpu.SemaphoreType.DMA((SIDE,)),
        ],
        compiler_params=pltpu.CompilerParams(collective_id=2, has_side_effects=True),
        name="head_sum",
    )(part)


def pack_weight(block, lane_chunks, rows):
    height, width = block.shape
    block = jnp.pad(block, ((0, 0), (0, lane_chunks * LANES - width)))
    block = block.reshape(height, lane_chunks, LANES).transpose(1, 0, 2)
    block = block.reshape(lane_chunks * height, LANES)
    block = jnp.pad(block, ((0, 2 * rows - lane_chunks * height), (0, 0)))
    return block.reshape(2, rows, LANES)


def unpack_weight(buf, lane_chunks, height, width):
    rows = buf.shape[4]
    count = SIDE * SIDE * SIDE
    buf = buf.reshape(2, count, rows, LANES).transpose(1, 0, 2, 3)
    buf = buf.reshape(count, 2 * rows, LANES)[:, : lane_chunks * height]
    buf = buf.reshape(count, lane_chunks, height, LANES).transpose(0, 2, 1, 3)
    return buf.reshape(count * height, lane_chunks * LANES)[:, :width]


def project(hidden_in, norm_gain, weight):
    tok_rows = hidden_in.shape[0]
    float_rows = hidden_in.astype(jnp.float32)
    normed = (
        float_rows
        * lax.rsqrt(jnp.mean(float_rows * float_rows, axis=-1, keepdims=True) + NORM_EPS)
        * norm_gain
    ).astype(jnp.bfloat16)
    projected = lax.dot_general(
        weight, normed, (((0,), (1,)), ((), ())), preferred_element_type=jnp.float32
    ).reshape(QPK + 2, HD, tok_rows)
    half = HD // 2
    frequency = ROPE_BASE ** (-2.0 * jnp.arange(half, dtype=jnp.float32) / HD)
    positions = lax.axis_index("tok") * tok_rows + jnp.arange(tok_rows, dtype=jnp.int32)
    angles = frequency[:, None] * positions.astype(jnp.float32)[None, :]
    cosine, sines = jnp.cos(angles)[None], jnp.sin(angles)[None]
    front, back = projected[: QPK + 1, :half], projected[: QPK + 1, half:]
    turned = jnp.concatenate(
        [front * cosine - back * sines, back * cosine + front * sines], axis=1
    ).astype(jnp.bfloat16)
    query = turned[:QPK].transpose(1, 0, 2).reshape(HD, QPK * tok_rows)
    key_value = jnp.concatenate([turned[QPK], projected[QPK + 1].astype(jnp.bfloat16)], axis=0)
    key_value = key_value.reshape(2 * HD, 2, LANES).transpose(1, 0, 2)
    return query, key_value


def outgoing_blocks(prefill_cache, lengths, prefill_table, decode_table):
    tok_count = lax.axis_size("tok")
    my_index = lax.axis_index("tok")
    layers, slot_count, _, extent = prefill_cache.shape
    block_total = prefill_table.shape[0]
    per_request = block_total // lengths.shape[0]
    every_block = jnp.arange(block_total, dtype=jnp.int32)
    slots = jnp.arange(slot_count, dtype=jnp.int32)
    mine = prefill_table[:, None] == (my_index * slot_count + slots)[None, :]
    held_here = jnp.sum(jnp.where(mine, every_block[:, None], 0), axis=0)
    target = jnp.sum(jnp.where(mine, (decode_table // slot_count)[:, None], 0), axis=0)
    request = held_here // per_request
    requests = jnp.arange(lengths.shape[0], dtype=jnp.int32)
    request_len = jnp.sum(
        jnp.where(request[:, None] == requests[None, :], lengths[None, :], 0), axis=1
    )
    first_token = held_here % per_request * BLK
    live = first_token[:, None] + jnp.arange(BLK, dtype=jnp.int32)[None, :] < request_len[:, None]
    peers = jnp.arange(tok_count, dtype=jnp.int32)
    slot_of = jnp.sum(jnp.where(target[None, :] == peers[:, None], slots[None, :], 0), axis=1)
    origin = (my_index - (target - my_index)) % tok_count
    blocks = prefill_cache.reshape(layers, slot_count, BLK, extent // BLK)
    blocks = jnp.where(live[None, :, :, None], blocks, jnp.zeros_like(blocks))
    blocks = blocks.reshape(layers, slot_count, extent).transpose(1, 0, 2)
    blocks = jnp.take(blocks, slot_of, axis=0)
    blocks = blocks.reshape(SIDE, SIDE, SIDE, layers, extent)
    return (blocks[..., :NEAR], blocks[..., NEAR:]), origin


def on_device(
    hidden_in, norm_gain, w_qkv, w_out, prefill_cache, lengths, prefill_table, decode_table
):
    layers, slot_count, kv_local, extent = prefill_cache.shape
    (near, far), origin = outgoing_blocks(
        prefill_cache, lengths, prefill_table, decode_table
    )
    weights, near, far = gather_tok(pack_weight(w_qkv, 4, 80), near, far, 48)
    query, key_value = project(hidden_in, norm_gain, unpack_weight(weights, 4, *w_qkv.shape))
    context, out_all, *arrived = attend(
        query, key_value, pack_weight(w_out.T, 3, 64), near, far
    )
    out_weight = unpack_weight(out_all, 3, w_out.shape[1], w_out.shape[0])
    part = jnp.dot(out_weight, context, preferred_element_type=jnp.float32).astype(jnp.bfloat16)
    heads = lax.axis_size("head")
    part = part.reshape(heads // 2, 2, part.shape[0] // heads, part.shape[1])
    attn_out = head_sum(part).T
    arrived = jnp.concatenate(arrived, axis=-1).reshape(slot_count, layers, extent)
    decode_cache = jnp.take(arrived, origin, axis=0).transpose(1, 0, 2)
    return attn_out, decode_cache.reshape(prefill_cache.shape)


def solution(mesh):
    in_specs = (
        P("tok", None),
        P(),
        P("tok", "head"),
        P("head", "tok"),
        P(None, "tok", "head", None),
        P(),
        P(),
        P(),
    )
    out_specs = (P("tok", "head"), P(None, "tok", "head", None))
    return jax.shard_map(
        on_device, mesh=mesh, in_specs=in_specs, out_specs=out_specs, check_vma=False
    )
```
